256 devices in a mesh: rows: 16 (over z_lo, y, core), cols: 16 (over x, z_hi).
Axes of the slice: x: 4, y: 4, z: 8 (z_hi: 4, z_lo: 2; z = z_hi * 2 + z_lo), core: 2. Of those that a mesh axis runs over, the one named last changes fastest.
Arguments:
- displacement: float32 [16384, 288], P(('rows', 'cols')), may hold values from -6 to 6
- positions: float32 [16384, 288], P(('rows', 'cols')), as said below
- cluster_basis: bfloat16 [16384, 288, 64], P(('rows', 'cols')), may hold values from -0.375 to 0.375
- near_pairs: int32 [65536, 2], P(('rows', 'cols')), may hold values from 0 to 67, as said below
- near_count: int32 [256], P(('rows', 'cols')), may hold values from 64 to 256, as said below
- far_pairs: int32 [262144, 2], P(('rows', 'cols')), may hold values from 0 to 1023, as said below
- far_count: int32 [256], P(('rows', 'cols')), may hold values from 256 to 1024, as said below
- far_blocks: bfloat16 [262144, 64, 64], P(('rows', 'cols')), may hold values from -0.75 to 0.75
- intact: int32 [16384, 96], P(('rows', 'cols')), may hold values 0 or 1
- stiffness: float32 [16384, 96], P(('rows', 'cols')), may hold values from 0.5 to 2
Outputs:
- net_traction: float32 [16384, 288], P(('rows', 'cols'))
- damage: float32 [16384, 96], P(('rows', 'cols'))
The draws below stay inside these ranges and needn't reach their ends.
Inputs may be any that keep to these rules, and one draw needn't show every extreme that they name: `positions`: centroids of the elements of each cluster. `near_pairs`: column 0 is a cluster of the device's own 64; column 1 counts from 2 clusters before the device's first cluster and names a cluster at most 2 away from the target in the cluster order. Dead slots hold valid entries too. `near_count`: loads differ from device to device. `far_pairs`: column 0 is a target cluster of the device's index along rows (0 to 1023); column 1 a source cluster of its index along cols (0 to 1023), numbered through the devices of that column in the order of rows. Dead slots hold valid entries too. `far_count`: loads differ from device to device.
All inputs are finite; a program needn't handle non-finite values. No bound on the sum of `intact` on one device may be relied on, other than what follows from the above.
Results may differ from the reference program's by a relative error of at most 0.0014.
Values may be sent and summed in bfloat16 or wider, within the bound.
A program may use at most 128 MiB of HBM per device.

```python
import math
import jax
import jax.numpy as jnp
from jax import lax

ELEMS = 96
RANK = 64
HALO = 2
CLUSTERS_DEV = 64
NEAR_MAX = 256
FAR_MAX = 1024
CLUSTERS = 16384
ROW_BLOCK = 1024
COL_BLOCK = 1024
N_ROWS = 16
N_COLS = 16
DEVICES = 256


def draw_positions(key, part):
    unit_key = jax.random.fold_in(key, 31)
    unit = jax.random.uniform(unit_key, (CLUSTERS, 3, ELEMS), jnp.float32, -1.0, 1.0)
    order = (jnp.arange(CLUSTERS, dtype=jnp.int32) % 4096).astype(jnp.float32)
    along_x = 0.6 * order[:, None] + 0.9 * unit[:, 0]
    along_y = 2.5 * unit[:, 1]
    along_z = 0.4 * unit[:, 2]
    return jnp.stack([along_x, along_y, along_z], axis=1).reshape(CLUSTERS, 3 * ELEMS)


def skewed_counts(key, largest):
    smallest = largest // 4
    spread_key, pick_key = jax.random.split(key)
    spread = jax.random.randint(spread_key, (DEVICES,), 0, largest - smallest + 1)
    counts = smallest + spread * spread // (largest - smallest)
    chosen = jax.random.randint(pick_key, (), 0, DEVICES)
    return jnp.where(jnp.arange(DEVICES, dtype=jnp.int32) == chosen, largest, counts).astype(jnp.int32)


def draw_near_count(key, part):
    return skewed_counts(jax.random.fold_in(key, 11), NEAR_MAX)


def draw_far_count(key, part):
    return skewed_counts(jax.random.fold_in(key, 12), FAR_MAX)


def draw_near_pairs(key, part):
    base_key = jax.random.fold_in(key, 21)
    target_key, shift_key, rim_key, reach_key = jax.random.split(base_key, 4)
    targets = jax.random.randint(target_key, (DEVICES, NEAR_MAX), 0, CLUSTERS_DEV)
    shifts = jax.random.randint(shift_key, (DEVICES, NEAR_MAX), -HALO, HALO + 1)
    rim = jax.random.randint(rim_key, (DEVICES, 4), 0, 2)
    raw_reach = jax.random.randint(reach_key, (DEVICES, 4), 0, 1024)
    reach = raw_reach % (HALO - rim)
    is_upper = jnp.arange(4, dtype=jnp.int32)[None, :] >= 2
    edge_targets = jnp.where(is_upper, CLUSTERS_DEV - 1 - rim, rim)
    edge_shifts = jnp.where(is_upper, HALO - reach, -HALO + reach)
    targets = targets.at[:, :4].set(edge_targets)
    shifts = shifts.at[:, :4].set(edge_shifts)
    sources = targets + HALO + shifts
    return jnp.stack([targets, sources], axis=-1).reshape(DEVICES * NEAR_MAX, 2).astype(jnp.int32)


def draw_far_pairs(key, part):
    base_key = jax.random.fold_in(key, 22)
    target_key, source_key = jax.random.split(base_key)
    targets = jax.random.randint(target_key, (DEVICES, FAR_MAX), 0, ROW_BLOCK)
    sources = jax.random.randint(source_key, (DEVICES, FAR_MAX), 0, COL_BLOCK)
    return jnp.stack([targets, sources], axis=-1).reshape(DEVICES * FAR_MAX, 2).astype(jnp.int32)


def plant(entries, stream_key, low, high):
    longest = entries.shape.index(max(entries.shape))
    spots = []
    for shift in (0, 1):
        where = [jax.random.randint(jax.random.fold_in(stream_key, axis), (), 0, length) for axis, length in enumerate(entries.shape)]
        where[longest] = (where[longest] + shift) % entries.shape[longest]
        spots.append(tuple(where))
    return entries.at[spots[0]].set(low).at[spots[1]].set(high)


def block_levels(rng, shape, cuts, low, high):
    gain = 1.0
    for position, blocks in cuts:
        steps = jax.random.uniform(jax.random.fold_in(jax.random.fold_in(rng, 6), position), (blocks,), jnp.float32, low / len(cuts), high / len(cuts))
        gain = gain * jnp.repeat(jnp.exp(steps), shape[position] // blocks).reshape((-1,) + (1,) * (len(shape) - 1 - position))
    return gain


def gaussian(rng, shape, scale, most, shards=(), kind=jnp.bfloat16):
    gain = block_levels(rng, shape, shards, -0.22, 0.18) if shards else 1.0
    values = jax.random.normal(rng, shape, jnp.float32) * scale * gain
    return jnp.minimum(jnp.maximum(values, -most), most).astype(kind)


def setup_inputs(seed: int = 0) -> dict:
    key_of = jax.random.split(jax.random.key(seed), 11)
    displacement = gaussian(key_of[0], (CLUSTERS, 3 * ELEMS), 1.0, 6.0, ((0, 256),), jnp.float32)
    positions = draw_positions(jax.random.fold_in(key_of[10], 71), 0)
    cluster_basis = gaussian(key_of[2], (CLUSTERS, 3 * ELEMS, RANK), (3 * ELEMS) ** -0.5, 0.375, ((0, 256),))
    near_pairs = draw_near_pairs(jax.random.fold_in(key_of[10], 71), 0)
    near_count = draw_near_count(jax.random.fold_in(key_of[10], 71), 0)
    far_pairs = draw_far_pairs(jax.random.fold_in(key_of[10], 71), 0)
    far_count = draw_far_count(jax.random.fold_in(key_of[10], 71), 0)
    far_blocks = gaussian(key_of[7], (N_ROWS * N_COLS * FAR_MAX, RANK, RANK), RANK ** -0.5, 0.75, ((0, 256),))
    intact = plant((jax.random.randint(key_of[8], (CLUSTERS, ELEMS), 0, 4) < 3).astype(jnp.int32), jax.random.fold_in(key_of[8], 1), 0, 1)
    stiffness = jnp.clip(jnp.exp(math.log(2.0) - 1.3862944 * jax.random.uniform(key_of[9], (CLUSTERS, ELEMS), jnp.float32) ** block_levels(key_of[9], (CLUSTERS, ELEMS), ((0, 256),), -0.2, 0.2)), 0.5, 2.0)
    return dict(displacement=displacement, positions=positions, cluster_basis=cluster_basis, near_pairs=near_pairs, near_count=near_count, far_pairs=far_pairs, far_count=far_count, far_blocks=far_blocks, intact=intact, stiffness=stiffness)


core_square = 0.25
softening = 1.5

def kernel_block(target_pos, source_pos, source_disp):
    offsets = target_pos[:, :, :, None] - source_pos[:, :, None, :]
    distance = lax.optimization_barrier(jnp.sum(offsets * offsets, axis=1)) + core_square
    inverse = lax.rsqrt(distance)
    inverse = inverse * inverse * inverse
    along = lax.optimization_barrier(jnp.sum(offsets * source_disp[:, :, None, :], axis=1))
    direct = lax.optimization_barrier(jnp.sum(inverse[:, None, :, :] * source_disp[:, :, None, :], axis=3))
    second = lax.optimization_barrier(jnp.sum(offsets * (along * inverse / distance)[:, None, :, :], axis=3))
    return direct - 3.0 * second

def reference(displacement, positions, cluster_basis, near_pairs, near_count, far_pairs, far_count, far_blocks, intact, stiffness):
    devices = N_ROWS * N_COLS
    clusters = CLUSTERS_DEV * devices
    row_width = 3 * ELEMS
    row_clusters = CLUSTERS_DEV * N_COLS
    padding = jnp.zeros((HALO, row_width), jnp.float32)
    ext_disp = jnp.concatenate([padding, displacement, padding], axis=0)
    ext_pos = jnp.concatenate([padding, positions, padding], axis=0)
    device_ids = jnp.arange(devices, dtype=jnp.int32)
    near_lists = near_pairs.reshape(devices, NEAR_MAX, 2)
    near_slots = jnp.arange(NEAR_MAX, dtype=jnp.int32)

    def near_device(summed, inputs):
        pair_list, slot_count, device = inputs
        first_cluster = device * CLUSTERS_DEV
        targets = first_cluster + pair_list[:, 0]
        sources = first_cluster + pair_list[:, 1]
        active = (near_slots < slot_count).astype(jnp.float32)
        target_pos = positions[targets].reshape(NEAR_MAX, 3, ELEMS)
        source_pos = ext_pos[sources].reshape(NEAR_MAX, 3, ELEMS)
        source_disp = ext_disp[sources].reshape(NEAR_MAX, 3, ELEMS)
        contrib = kernel_block(target_pos, source_pos, source_disp) * active[:, None, None]
        return (summed.at[targets].add(contrib.reshape(NEAR_MAX, row_width)), None)
    near_sum = lax.scan(near_device, jnp.zeros((clusters, row_width), jnp.float32), (near_lists, near_count, device_ids))[0]
    basis_dev = cluster_basis.reshape(devices, CLUSTERS_DEV, row_width, RANK)
    disp_dev = displacement.astype(jnp.bfloat16).reshape(devices, CLUSTERS_DEV, row_width)

    def project(inputs):
        local_basis, local_disp = inputs
        result = jnp.einsum('kf,kfr->kr', local_disp.astype(jnp.float32), local_basis.astype(jnp.float32))
        return result.astype(jnp.bfloat16)
    coeff_bf = lax.map(project, (basis_dev, disp_dev)).reshape(clusters, RANK)
    far_lists = far_pairs.reshape(devices, FAR_MAX, 2)
    blocks_dev = far_blocks.reshape(devices, FAR_MAX, RANK, RANK)
    far_slots = jnp.arange(FAR_MAX, dtype=jnp.int32)

    def far_device(summed, inputs):
        pair_list, slot_count, blocks, device = inputs
        row_index = device // N_COLS
        col_index = device % N_COLS
        targets = row_index * row_clusters + pair_list[:, 0]
        local = pair_list[:, 1]
        sources = local // CLUSTERS_DEV * row_clusters + col_index * CLUSTERS_DEV + local % CLUSTERS_DEV
        active = (far_slots < slot_count).astype(jnp.float32)
        coupled = jnp.einsum('prs,ps->pr', blocks.astype(jnp.float32), coeff_bf[sources].astype(jnp.float32))
        return (summed.at[targets].add(coupled * active[:, None]), None)
    coupled_sum = lax.scan(far_device, jnp.zeros((clusters, RANK), jnp.float32), (far_lists, far_count, blocks_dev, device_ids))[0]
    coupled_dev = coupled_sum.astype(jnp.bfloat16).reshape(devices, CLUSTERS_DEV, RANK)

    def expand(inputs):
        local_basis, local_coupled = inputs
        return jnp.einsum('kfr,kr->kf', local_basis.astype(jnp.float32), local_coupled.astype(jnp.float32))
    far_part = lax.map(expand, (basis_dev, coupled_dev)).reshape(clusters, row_width)
    traction = near_sum + far_part
    disp3 = displacement.reshape(clusters, 3, ELEMS)
    separation = jnp.sqrt(1.0 + lax.optimization_barrier(jnp.sum(disp3 * disp3, axis=1)))
    softened = 1.0 - jnp.exp(-(separation - 1.0) / softening)
    intact_float = intact.astype(jnp.float32)
    damage = intact_float * softened + (1.0 - intact_float)
    holding = ((1.0 - damage) * stiffness)[:, None, :] * disp3
    net_traction = traction - holding.reshape(clusters, row_width)
    return (net_traction, damage)
```

```python
import functools

import jax
import jax.numpy as jnp
from jax import lax
from jax.experimental import pallas as pl
from jax.experimental.pallas import tpu as pltpu
from jax.sharding import PartitionSpec as P

MESH = pl.DeviceIdType.MESH
ELEMS = 96
RANK = 64
OWN = 64
WIDTH = 3 * ELEMS
LANES = 128
GROUPS = OWN // 4
core_square = 0.25
softening = 1.5

FIRST = (1, 6)
SECOND = (6, 11)
THIRD = (11, 15)


def mega(
    n_rows,
    n_cols,
    coeff,
    disp,
    pos,
    near_pairs,
    near_count,
    far_pairs,
    far_count,
    far_hbm,
    near_out,
    owned_out,
    ext_disp,
    ext_pos,
    turned,
    wide,
    targets,
    weights,
    near_sum,
    far_blocks,
    column,
    coupled,
    split,
    partial,
    arrived,
    far_sem,
    halo_send,
    halo_recv,
    gather_send,
    gather_recv,
    scatter_send,
    scatter_recv,
):
    f32, bf16 = jnp.float32, jnp.bfloat16
    i, j = lax.axis_index("rows"), lax.axis_index("cols")
    me = i * n_cols + j
    devices = n_rows * n_cols
    after = (me + 1) % devices
    before = (me + devices - 1) % devices
    next_id = (after // n_cols, after % n_cols)
    last_id = (before // n_cols, before % n_cols)
    row_peers = [((i + d) % n_rows, j) for d in range(1, n_rows)]
    col_peers = [(i, (j + d) % n_cols) for d in range(1, n_cols)]

    far_copy = pltpu.make_async_copy(far_hbm, far_blocks, far_sem)
    far_copy.start()
    barrier = pltpu.get_barrier_semaphore()
    peers = row_peers + col_peers + [next_id, last_id]
    for peer in peers:
        pl.semaphore_signal(barrier, inc=1, device_id=peer, device_id_type=MESH)

    ext_disp[0:OWN, :] = disp[...]
    ext_pos[0:OWN, :] = pos[...]

    def turn(rows):
        for c in range(3):
            lanes = slice(c * ELEMS, (c + 1) * ELEMS)
            turned[c, :, 0:rows] = ext_pos[0:rows, lanes].T
            turned[3 + c, :, 0:rows] = ext_disp[0:rows, lanes].T

    turn(OWN)
    for c in range(3):
        wide[:, 0:ELEMS] = pos[:, c * ELEMS : (c + 1) * ELEMS]
        a0, a1, a2, a3 = [wide[pl.ds(m, GROUPS, stride=4), :][:, :ELEMS] for m in range(4)]
        targets[c, 0] = jnp.concatenate([a0, a1[:, :32]], axis=1)
        targets[c, 1] = jnp.concatenate([a1[:, 32:], a2[:, :64]], axis=1)
        targets[c, 2] = jnp.concatenate([a2[:, 64:], a3], axis=1)

    slots = near_pairs.shape[1]
    near_target = near_pairs[0:1, :]
    near_source = near_pairs[1:2, :]
    group = near_target // 4
    live = lax.broadcasted_iota(jnp.int32, (1, slots), 1) < near_count[0]
    row = jnp.where(live, group * 8 + near_source - group * 4, -1)
    place = near_target - group * 4
    row_is = (lax.broadcasted_iota(jnp.int32, (8 * GROUPS, slots), 0) == row).astype(f32)
    lane_is = (lax.broadcasted_iota(jnp.int32, (4 * ELEMS, slots), 0) // ELEMS == place).astype(f32)
    for v in range(3):
        weights[v] = lax.dot_general(
            row_is.astype(bf16),
            lane_is[v * LANES : (v + 1) * LANES].astype(bf16),
            (((1,), (1,)), ((), ())),
            preferred_element_type=f32,
        )

    def near_group(g, _):
        shift = (130 - 4 * g) % LANES
        xs = [[jnp.broadcast_to(targets[c, v, pl.ds(g, 1), :], (8, LANES)) for c in range(3)] for v in range(3)]

        def step(part, totals):
            totals = [list(t) for t in totals]
            first = pl.multiple_of(part * 8, 8)
            tiles = [pltpu.roll(turned[q, pl.ds(first, 8), :], shift, axis=1) for q in range(6)]
            for s in range(8):
                y = [jnp.broadcast_to(tiles[c][:, s : s + 1], (8, LANES)) for c in range(3)]
                u = [jnp.broadcast_to(tiles[3 + c][:, s : s + 1], (8, LANES)) for c in range(3)]
                for v in range(3):
                    if not v <= s <= v + 5:
                        continue
                    r = [xs[v][c] - y[c] for c in range(3)]
                    q = (r[0] * r[0] + r[1] * r[1]) + (r[2] * r[2] + core_square)
                    inverse = lax.rsqrt(q)
                    square = inverse * inverse
                    count = jnp.broadcast_to(weights[v, pl.ds(8 * g + s, 1), :], (8, LANES))
                    cube = (square * inverse) * count
                    along = (r[0] * u[0] + r[1] * u[1] + r[2] * u[2]) * (3.0 * square)
                    for c in range(3):
                        totals[v][c] = totals[v][c] + cube * (u[c] - along * r[c])
            return totals

        zero = [[jnp.zeros((8, LANES), f32) for _ in range(3)] for _ in range(3)]
        totals = lax.fori_loop(0, ELEMS // 8, step, zero)
        for v in range(3):
            for c in range(3):
                near_sum[c, v, pl.ds(g, 1), :] = jnp.sum(totals[v][c], axis=0, keepdims=True)
        return 0

    lax.fori_loop(*FIRST, near_group, 0)
    pl.semaphore_wait(barrier, len(peers))

    def remote(src, dst, send, recv, peer):
        return pltpu.make_async_remote_copy(
            src_ref=src, dst_ref=dst, send_sem=send, recv_sem=recv, device_id=peer, device_id_type=MESH
        )

    mine = column.at[pl.ds(pl.multiple_of(i * OWN, OWN), OWN), :]
    gathers = [
        remote(coeff, mine, gather_send.at[d], gather_recv.at[d], peer) for d, peer in enumerate(row_peers)
    ]
    halos = []
    for n, (src, dst) in enumerate(((disp, ext_disp), (pos, ext_pos))):
        halos.append(remote(src.at[pl.ds(OWN - 8, 8), :], dst.at[pl.ds(120, 8), :], halo_send.at[n], halo_recv.at[n], next_id))
        halos.append(remote(src.at[pl.ds(0, 8), :], dst.at[pl.ds(OWN, 8), :], halo_send.at[2 + n], halo_recv.at[2 + n], last_id))
    for copy in gathers + halos:
        copy.start()
    column[pl.ds(pl.multiple_of(i * OWN, OWN), OWN), :] = coeff[...]

    lax.fori_loop(*SECOND, near_group, 0)

    for copy in gathers:
        copy.wait()
    far_copy.wait()
    column_turned = column[...].astype(f32).T.astype(bf16)
    far_slots = far_pairs.shape[1]
    sources = n_rows * OWN

    def couple(block, _):
        first = pl.multiple_of(block * LANES, LANES)
        source = far_pairs[1:2, pl.ds(first, LANES)]
        alive = lax.broadcasted_iota(jnp.int32, (1, LANES), 1) + first < far_count[0]
        source = jnp.where(alive, source, -1)
        chosen = (lax.broadcasted_iota(jnp.int32, (sources, LANES), 0) == source).astype(f32).astype(bf16)
        gathered = jnp.dot(column_turned, chosen, preferred_element_type=f32)

        def ranks(part, _):
            top = pl.multiple_of(part * 8, 8)
            blocks = far_blocks[pl.ds(top, 8), :, pl.ds(first, LANES)].astype(f32)
            coupled[pl.ds(top, 8), pl.ds(first, LANES)] = jnp.sum(blocks * gathered[None], axis=1)
            return 0

        return lax.fori_loop(0, RANK // 8, ranks, 0)

    lax.fori_loop(0, far_slots // LANES, couple, 0)
    whole = coupled[...]
    high = whole.astype(bf16)
    split[0:RANK, :] = high
    split[RANK : 2 * RANK, :] = (whole - high.astype(f32)).astype(bf16)

    def collect(block, _):
        first = pl.multiple_of(block * LANES, LANES)
        chosen = (lax.broadcasted_iota(jnp.int32, (LANES, far_slots), 0) + first == far_pairs[0:1, :]).astype(f32)
        both = lax.dot_general(
            chosen.astype(bf16), split[...], (((1,), (1,)), ((), ())), preferred_element_type=f32
        )
        partial[pl.ds(first, LANES), :] = (both[:, :RANK] + both[:, RANK:]).astype(bf16)
        return 0

    lax.fori_loop(0, n_cols * OWN // LANES, collect, 0)

    for copy in halos:
        copy.wait()

    here = pl.ds(pl.multiple_of(j * OWN, OWN), OWN)
    scatters = []
    for d, peer in enumerate(col_peers):
        block = partial.at[pl.ds(pl.multiple_of(peer[1] * OWN, OWN), OWN), :]
        scatters.append(remote(block, arrived.at[here, :], scatter_send.at[d], scatter_recv.at[d], peer))
    for copy in scatters:
        copy.start()
    arrived[here, :] = partial[here, :]

    ext_disp[OWN : OWN + 8, :] = jnp.where(me == devices - 1, 0.0, ext_disp[OWN : OWN + 8, :])
    ext_disp[120:128, :] = jnp.where(me == 0, 0.0, ext_disp[120:128, :])
    turn(2 * OWN)
    lax.fori_loop(*THIRD, near_group, 0)
    near_group(0, 0)
    near_group(GROUPS - 1, 0)

    quarters = [[], [], [], []]
    for c in range(3):
        v0, v1, v2 = [near_sum[c, v] for v in range(3)]
        quarters[0].append(v0[:, :96])
        quarters[1].append(jnp.concatenate([v0[:, 96:], v1[:, :64]], axis=1))
        quarters[2].append(jnp.concatenate([v1[:, 64:], v2[:, :32]], axis=1))
        quarters[3].append(v2[:, 32:])
    for m in range(4):
        near_out[m] = jnp.concatenate(quarters[m], axis=1)

    for copy in scatters:
        copy.wait()
    owned = arrived[0:OWN, :].astype(f32)
    for n in range(1, n_cols):
        owned = owned + arrived[n * OWN : (n + 1) * OWN, :].astype(f32)
    owned_out[...] = owned.astype(bf16)


def local(
    displacement,
    positions,
    cluster_basis,
    near_pairs,
    near_count,
    far_pairs,
    far_count,
    far_blocks,
    intact,
    stiffness,
):
    n_rows, n_cols = lax.axis_size("rows"), lax.axis_size("cols")
    f32, bf16 = jnp.float32, jnp.bfloat16
    disp_bf = displacement.astype(bf16)
    coeff = jnp.einsum("kf,kfr->kr", disp_bf, cluster_basis, preferred_element_type=f32).astype(bf16)
    far_slots = far_pairs.shape[0]
    vmem = pl.BlockSpec(memory_space=pltpu.VMEM)
    smem = pl.BlockSpec(memory_space=pltpu.SMEM)
    near, owned = pl.pallas_call(
        functools.partial(mega, n_rows, n_cols),
        out_shape=(
            jax.ShapeDtypeStruct((4, GROUPS, WIDTH), f32),
            jax.ShapeDtypeStruct((OWN, RANK), bf16),
        ),
        in_specs=[vmem, vmem, vmem, vmem, smem, vmem, smem, pl.BlockSpec(memory_space=pl.ANY)],
        out_specs=(vmem, vmem),
        scratch_shapes=[
            pltpu.VMEM((2 * OWN, WIDTH), f32),
            pltpu.VMEM((2 * OWN, WIDTH), f32),
            pltpu.VMEM((6, ELEMS, LANES), f32),
            pltpu.VMEM((OWN, LANES), f32),
            pltpu.VMEM((3, 3, GROUPS, LANES), f32),
            pltpu.VMEM((3, 8 * GROUPS, LANES), f32),
            pltpu.VMEM((3, 3, GROUPS, LANES), f32),
            pltpu.VMEM((RANK, RANK, far_slots), bf16),
            pltpu.VMEM((n_rows * OWN, RANK), bf16),
            pltpu.VMEM((RANK, far_slots), f32),
            pltpu.VMEM((2 * RANK, far_slots), bf16),
            pltpu.VMEM((n_cols * OWN, RANK), bf16),
            pltpu.VMEM((n_cols * OWN, RANK), bf16),
            pltpu.SemaphoreType.DMA,
            pltpu.SemaphoreType.DMA((4,)),
            pltpu.SemaphoreType.DMA((4,)),
            pltpu.SemaphoreType.DMA((n_rows - 1,)),
            pltpu.SemaphoreType.DMA((n_rows - 1,)),
            pltpu.SemaphoreType.DMA((n_cols - 1,)),
            pltpu.SemaphoreType.DMA((n_cols - 1,)),
        ],
        compiler_params=pltpu.CompilerParams(
            collective_id=0, has_side_effects=True, vmem_limit_bytes=40 * 1024 * 1024
        ),
        name="traction",
    )(
        coeff,
        displacement,
        positions,
        near_pairs.T,
        near_count,
        far_pairs.T,
        far_count,
        jnp.transpose(far_blocks, (1, 2, 0)),
    )
    near_sum = jnp.swapaxes(near, 0, 1).reshape(OWN, WIDTH)
    far_part = jnp.einsum("kfr,kr->kf", cluster_basis, owned, preferred_element_type=f32)
    traction = near_sum + far_part
    disp3 = displacement.reshape(OWN, 3, ELEMS)
    separation = jnp.sqrt(1.0 + jnp.sum(disp3 * disp3, axis=1))
    softened = 1.0 - jnp.exp(-(separation - 1.0) / softening)
    intact_float = intact.astype(f32)
    damage = intact_float * softened + (1.0 - intact_float)
    holding = ((1.0 - damage) * stiffness)[:, None, :] * disp3
    net_traction = traction - holding.reshape(OWN, WIDTH)
    return (net_traction, damage)


def solution(mesh):
    both = ("rows", "cols")
    in_specs = (
        P(both, None),
        P(both, None),
        P(both, None, None),
        P(both, None),
        P(both),
        P(both, None),
        P(both),
        P(both, None, None),
        P(both, None),
        P(both, None),
    )
    out_specs = (P(both, None), P(both, None))
    return jax.shard_map(local, mesh=mesh, in_specs=in_specs, out_specs=out_specs, check_vma=False)
```

```python
import functools

import jax
import jax.numpy as jnp
from jax import lax
from jax.experimental import pallas as pl
from jax.experimental.pallas import tpu as pltpu
from jax.sharding import PartitionSpec as P

MESH = pl.DeviceIdType.MESH
ELEMS = 96
RANK = 64
OWN = 64
WIDTH = 3 * ELEMS
LANES = 128
GROUPS = OWN // 4
core_square = 0.25
softening = 1.5

FIRST = (1, 6)
SECOND = (6, 11)
THIRD = (11, 16)


def mega(
    n_rows,
    n_cols,
    disp,
    pos,
    near_pairs,
    near_count,
    far_pairs,
    far_count,
    intact,
    stiffness,
    basis_hbm,
    far_hbm,
    base_out,
    damage_out,
    owned_out,
    ext_disp,
    ext_pos,
    turned,
    wide,
    targets,
    weights,
    spread,
    near_sum,
    near_rows,
    basis,
    far_blocks,
    column,
    coupled,
    split,
    partial,
    arrived,
    basis_sem,
    far_sem,
    halo_send,
    halo_recv,
    gather_send,
    gather_recv,
    scatter_send,
    scatter_recv,
):
    f32, bf16 = jnp.float32, jnp.bfloat16
    i, j = lax.axis_index("rows"), lax.axis_index("cols")
    me = i * n_cols + j
    devices = n_rows * n_cols
    after = (me + 1) % devices
    before = (me + devices - 1) % devices
    next_id = (after // n_cols, after % n_cols)
    last_id = (before // n_cols, before % n_cols)
    row_peers = [((i + d) % n_rows, j) for d in range(1, n_rows)]
    col_peers = [(i, (j + d) % n_cols) for d in range(1, n_cols)]

    basis_copy = pltpu.make_async_copy(basis_hbm, basis, basis_sem)
    basis_copy.start()
    far_copy = pltpu.make_async_copy(far_hbm, far_blocks, far_sem)
    far_copy.start()
    barrier = pltpu.get_barrier_semaphore()
    peers = row_peers + col_peers + [next_id, last_id]
    for peer in peers:
        pl.semaphore_signal(barrier, inc=1, device_id=peer, device_id_type=MESH)

    ext_disp[0:OWN, :] = disp[...]
    ext_pos[0:OWN, :] = pos[...]

    def turn(rows):
        for c in range(3):
            lanes = slice(c * ELEMS, (c + 1) * ELEMS)
            turned[c, :, 0:rows] = ext_pos[0:rows, lanes].T
            turned[3 + c, :, 0:rows] = ext_disp[0:rows, lanes].T

    turn(OWN)
    for c in range(3):
        wide[:, 0:ELEMS] = pos[:, c * ELEMS : (c + 1) * ELEMS]
        a0, a1, a2, a3 = [wide[pl.ds(m, GROUPS, stride=4), :][:, :ELEMS] for m in range(4)]
        targets[c, 0] = jnp.concatenate([a0, a1[:, :32]], axis=1)
        targets[c, 1] = jnp.concatenate([a1[:, 32:], a2[:, :64]], axis=1)
        targets[c, 2] = jnp.concatenate([a2[:, 64:], a3], axis=1)

    slots = near_pairs.shape[1]
    near_target = near_pairs[0:1, :]
    near_source = near_pairs[1:2, :]
    group = near_target // 4
    live = lax.broadcasted_iota(jnp.int32, (1, slots), 1) < near_count[0]
    row = jnp.where(live, group * 8 + near_source - group * 4, -1)
    place = near_target - group * 4
    row_is = (lax.broadcasted_iota(jnp.int32, (8 * GROUPS, slots), 0) == row).astype(f32)
    lane_is = (lax.broadcasted_iota(jnp.int32, (4 * ELEMS, slots), 0) // ELEMS == place).astype(f32)
    for v in range(3):
        weights[v] = lax.dot_general(
            row_is.astype(bf16),
            lane_is[v * LANES : (v + 1) * LANES].astype(bf16),
            (((1,), (1,)), ((), ())),
            preferred_element_type=f32,
        )

    def fill(buffer, g, part):
        shift = (130 - 4 * g) % LANES
        first = pl.multiple_of(part * 8, 8)
        for q in range(6):
            tile = pltpu.roll(turned[q, pl.ds(first, 8), :], shift, axis=1)
            for s in range(8):
                buffer[6 * s + q] = jnp.broadcast_to(tile[:, s : s + 1], (8, LANES))

    def interact(buffer, g, totals):
        totals = [list(t) for t in totals]
        xs = [[jnp.broadcast_to(targets[c, v, pl.ds(g, 1), :], (8, LANES)) for c in range(3)] for v in range(3)]
        for s in range(8):
            y = [buffer[6 * s + c] for c in range(3)]
            u = [buffer[6 * s + 3 + c] for c in range(3)]
            for v in range(3):
                if not v <= s <= v + 5:
                    continue
                r = [xs[v][c] - y[c] for c in range(3)]
                q = (r[0] * r[0] + r[1] * r[1]) + (r[2] * r[2] + core_square)
                inverse = lax.rsqrt(q)
                square = inverse * inverse
                count = jnp.broadcast_to(weights[v, pl.ds(8 * g + s, 1), :], (8, LANES))
                cube = (square * inverse) * count
                along = (r[0] * u[0] + r[1] * u[1] + r[2] * u[2]) * (3.0 * square)
                for c in range(3):
                    totals[v][c] = totals[v][c] + cube * (u[c] - along * r[c])
        return totals

    def near_groups(first, last):
        fill(spread, first, 0)

        def one(g, _):
            def one_part(p, totals):
                totals = interact(spread, g, totals)
                wrap = p == ELEMS // 8 - 1
                fill(spread, jnp.where(wrap, g + 1, g), jnp.where(wrap, 0, p + 1))
                return totals

            zero = [[jnp.zeros((8, LANES), f32) for _ in range(3)] for _ in range(3)]
            totals = lax.fori_loop(0, ELEMS // 8, one_part, zero)
            for v in range(3):
                for c in range(3):
                    near_sum[c, v, pl.ds(g, 1), :] = jnp.sum(totals[v][c], axis=0, keepdims=True)
            return 0

        lax.fori_loop(first, last, one, 0)

    basis_copy.wait()

    def project(block, coeff):
        top = pl.multiple_of(block * 8, 8)
        rows = disp[pl.ds(top, 8), :].astype(bf16).astype(f32)
        lane = lax.broadcasted_iota(jnp.int32, (RANK, OWN), 1)
        for n in range(8):
            product = basis[top + n].astype(f32) * rows[n : n + 1, :]
            coeff = jnp.where(lane == top + n, jnp.sum(product, axis=1, keepdims=True), coeff)
        return coeff

    coeff = lax.fori_loop(0, OWN // 8, project, jnp.zeros((RANK, OWN), f32))
    own_rows = pl.ds(pl.multiple_of(i * OWN, OWN), OWN)
    column[own_rows, :] = coeff.astype(bf16)

    near_groups(*FIRST)
    pl.semaphore_wait(barrier, len(peers))

    def remote(src, dst, send, recv, peer):
        return pltpu.make_async_remote_copy(
            src_ref=src, dst_ref=dst, send_sem=send, recv_sem=recv, device_id=peer, device_id_type=MESH
        )

    mine = column.at[own_rows, :]
    gathers = [
        remote(mine, mine, gather_send.at[d], gather_recv.at[d], peer) for d, peer in enumerate(row_peers)
    ]
    halos = []
    for n, (src, dst) in enumerate(((disp, ext_disp), (pos, ext_pos))):
        halos.append(remote(src.at[pl.ds(OWN - 8, 8), :], dst.at[pl.ds(120, 8), :], halo_send.at[n], halo_recv.at[n], next_id))
        halos.append(remote(src.at[pl.ds(0, 8), :], dst.at[pl.ds(OWN, 8), :], halo_send.at[2 + n], halo_recv.at[2 + n], last_id))
    for copy in gathers + halos:
        copy.start()

    near_groups(*SECOND)

    for copy in gathers:
        copy.wait()
    far_copy.wait()
    column_turned = jnp.concatenate([column[n * OWN : (n + 1) * OWN, :] for n in range(n_rows)], axis=1)
    far_slots = far_pairs.shape[1]
    sources = n_rows * OWN

    def couple(block, _):
        first = pl.multiple_of(block * LANES, LANES)
        source = far_pairs[1:2, pl.ds(first, LANES)]
        alive = lax.broadcasted_iota(jnp.int32, (1, LANES), 1) + first < far_count[0]
        source = jnp.where(alive, source, -1)
        chosen = (lax.broadcasted_iota(jnp.int32, (sources, LANES), 0) == source).astype(f32).astype(bf16)
        gathered = jnp.dot(column_turned, chosen, preferred_element_type=f32)

        def ranks(part, _):
            top = pl.multiple_of(part * 8, 8)
            blocks = far_blocks[pl.ds(top, 8), :, pl.ds(first, LANES)].astype(f32)
            coupled[pl.ds(top, 8), pl.ds(first, LANES)] = jnp.sum(blocks * gathered[None], axis=1)
            return 0

        return lax.fori_loop(0, RANK // 8, ranks, 0)

    lax.fori_loop(0, far_slots // LANES, couple, 0)
    whole = coupled[...]
    high = whole.astype(bf16)
    split[0:RANK, :] = high
    split[RANK : 2 * RANK, :] = (whole - high.astype(f32)).astype(bf16)

    def collect(block, _):
        first = pl.multiple_of(block * LANES, LANES)
        chosen = (lax.broadcasted_iota(jnp.int32, (LANES, far_slots), 0) + first == far_pairs[0:1, :]).astype(f32)
        both = lax.dot_general(
            chosen.astype(bf16), split[...], (((1,), (1,)), ((), ())), preferred_element_type=f32
        )
        partial[pl.ds(first, LANES), :] = (both[:, :RANK] + both[:, RANK:]).astype(bf16)
        return 0

    lax.fori_loop(0, n_cols * OWN // LANES, collect, 0)

    for copy in halos:
        copy.wait()

    here = pl.ds(pl.multiple_of(j * OWN, OWN), OWN)
    scatters = []
    for d, peer in enumerate(col_peers):
        block = partial.at[pl.ds(pl.multiple_of(peer[1] * OWN, OWN), OWN), :]
        scatters.append(remote(block, arrived.at[here, :], scatter_send.at[d], scatter_recv.at[d], peer))
    for copy in scatters:
        copy.start()
    arrived[here, :] = partial[here, :]

    ext_disp[OWN : OWN + 8, :] = jnp.where(me == devices - 1, 0.0, ext_disp[OWN : OWN + 8, :])
    ext_disp[120:128, :] = jnp.where(me == 0, 0.0, ext_disp[120:128, :])
    turn(2 * OWN)
    near_groups(*THIRD)
    near_groups(0, 1)

    parts = []
    for c in range(3):
        v0, v1, v2 = [near_sum[c, v] for v in range(3)]
        pad = jnp.zeros((GROUPS, LANES - ELEMS), f32)
        near_rows[pl.ds(0, GROUPS, stride=4), :] = v0
        near_rows[pl.ds(1, GROUPS, stride=4), :] = jnp.concatenate([v0[:, 96:], v1[:, :64], pad], axis=1)
        near_rows[pl.ds(2, GROUPS, stride=4), :] = jnp.concatenate([v1[:, 64:], v2[:, :32], pad], axis=1)
        near_rows[pl.ds(3, GROUPS, stride=4), :] = jnp.concatenate([v2[:, 32:], pad], axis=1)
        parts.append(near_rows[:, :ELEMS])
    u = [disp[:, c * ELEMS : (c + 1) * ELEMS] for c in range(3)]
    separation = jnp.sqrt(1.0 + (u[0] * u[0] + u[1] * u[1] + u[2] * u[2]))
    softened = 1.0 - jnp.exp(-(separation - 1.0) / softening)
    whole_element = intact[...].astype(f32)
    damage = whole_element * softened + (1.0 - whole_element)
    damage_out[...] = damage
    held = (1.0 - damage) * stiffness[...]
    base_out[...] = jnp.concatenate([parts[c] - held * u[c] for c in range(3)], axis=1)

    for copy in scatters:
        copy.wait()
    owned = arrived[0:OWN, :].astype(f32)
    for n in range(1, n_cols):
        owned = owned + arrived[n * OWN : (n + 1) * OWN, :].astype(f32)
    owned_out[...] = owned.astype(bf16)


def local(
    displacement,
    positions,
    cluster_basis,
    near_pairs,
    near_count,
    far_pairs,
    far_count,
    far_blocks,
    intact,
    stiffness,
):
    n_rows, n_cols = lax.axis_size("rows"), lax.axis_size("cols")
    f32, bf16 = jnp.float32, jnp.bfloat16
    far_slots = far_pairs.shape[0]
    vmem = pl.BlockSpec(memory_space=pltpu.VMEM)
    smem = pl.BlockSpec(memory_space=pltpu.SMEM)
    hbm = pl.BlockSpec(memory_space=pl.ANY)
    base, damage, owned = pl.pallas_call(
        functools.partial(mega, n_rows, n_cols),
        out_shape=(
            jax.ShapeDtypeStruct((OWN, WIDTH), f32),
            jax.ShapeDtypeStruct((OWN, ELEMS), f32),
            jax.ShapeDtypeStruct((OWN, RANK), bf16),
        ),
        in_specs=[vmem, vmem, vmem, smem, vmem, smem, vmem, vmem, hbm, hbm],
        out_specs=(vmem, vmem, vmem),
        scratch_shapes=[
            pltpu.VMEM((2 * OWN, WIDTH), f32),
            pltpu.VMEM((2 * OWN, WIDTH), f32),
            pltpu.VMEM((6, ELEMS, LANES), f32),
            pltpu.VMEM((OWN, LANES), f32),
            pltpu.VMEM((3, 3, GROUPS, LANES), f32),
            pltpu.VMEM((3, 8 * GROUPS, LANES), f32),
            pltpu.VMEM((48, 8, LANES), f32),
            pltpu.VMEM((3, 3, GROUPS, LANES), f32),
            pltpu.VMEM((OWN, LANES), f32),
            pltpu.VMEM((OWN, RANK, WIDTH), bf16),
            pltpu.VMEM((RANK, RANK, far_slots), bf16),
            pltpu.VMEM((n_rows * OWN, RANK), bf16),
            pltpu.VMEM((RANK, far_slots), f32),
            pltpu.VMEM((2 * RANK, far_slots), bf16),
            pltpu.VMEM((n_cols * OWN, RANK), bf16),
            pltpu.VMEM((n_cols * OWN, RANK), bf16),
            pltpu.SemaphoreType.DMA,
            pltpu.SemaphoreType.DMA,
            pltpu.SemaphoreType.DMA((4,)),
            pltpu.SemaphoreType.DMA((4,)),
            pltpu.SemaphoreType.DMA((n_rows - 1,)),
            pltpu.SemaphoreType.DMA((n_rows - 1,)),
            pltpu.SemaphoreType.DMA((n_cols - 1,)),
            pltpu.SemaphoreType.DMA((n_cols - 1,)),
        ],
        compiler_params=pltpu.CompilerParams(
            collective_id=0, has_side_effects=True, vmem_limit_bytes=40 * 1024 * 1024
        ),
        name="traction",
    )(
        displacement,
        positions,
        near_pairs.T,
        near_count,
        far_pairs.T,
        far_count,
        intact,
        stiffness,
        jnp.transpose(cluster_basis, (0, 2, 1)),
        jnp.transpose(far_blocks, (1, 2, 0)),
    )
    far_part = jnp.einsum("kfr,kr->kf", cluster_basis, owned, preferred_element_type=f32)
    return (base + far_part, damage)


def solution(mesh):
    both = ("rows", "cols")
    in_specs = (
        P(both, None),
        P(both, None),
        P(both, None, None),
        P(both, None),
        P(both),
        P(both, None),
        P(both),
        P(both, None, None),
        P(both, None),
        P(both, None),
    )
    out_specs = (P(both, None), P(both, None))
    return jax.shard_map(local, mesh=mesh, in_specs=in_specs, out_specs=out_specs, check_vma=False)
```

```python
import functools

import jax
import jax.numpy as jnp
from jax import lax
from jax.experimental import pallas as pl
from jax.experimental.pallas import tpu as pltpu
from jax.sharding import PartitionSpec as P

MESH = pl.DeviceIdType.MESH
ELEMS = 96
RANK = 64
OWN = 64
WIDTH = 3 * ELEMS
LANES = 128
GROUPS = OWN // 4
core_square = 0.25
softening = 1.5

PIECES = ((0, 0), (0, 1), (1, 0), (1, 1), (0, 2), (2, 0))
SEEN = (range(0, 4), range(0, 5), range(1, 6), range(2, 6))
FIRST = (1, 6)
SECOND = (6, 11)
THIRD = (11, 16)


def mega(
    n_rows,
    n_cols,
    near_count,
    far_count,
    disp_hbm,
    pos_hbm,
    near_pairs_hbm,
    far_pairs_hbm,
    intact_hbm,
    stiffness_hbm,
    basis_hbm,
    far_hbm,
    base_out,
    damage_out,
    owned_out,
    ext_disp,
    ext_pos,
    near_pairs,
    far_pairs,
    intact,
    stiffness,
    wide,
    centred,
    left,
    right_q,
    right_s,
    disp_rows,
    pos_rows,
    weights,
    near_rows,
    basis,
    far_blocks,
    column,
    coupled,
    split,
    partial,
    arrived,
    local_sem,
    halo_send,
    halo_recv,
    gather_send,
    gather_recv,
    scatter_send,
    scatter_recv,
):
    f32, bf16 = jnp.float32, jnp.bfloat16
    i, j = lax.axis_index("rows"), lax.axis_index("cols")
    me = i * n_cols + j
    devices = n_rows * n_cols
    after = (me + 1) % devices
    before = (me + devices - 1) % devices
    next_id = (after // n_cols, after % n_cols)
    last_id = (before // n_cols, before % n_cols)
    row_peers = [((i + d) % n_rows, j) for d in range(1, n_rows)]
    col_peers = [(i, (j + d) % n_cols) for d in range(1, n_cols)]

    own = pl.ds(0, OWN)
    loads = [
        pltpu.make_async_copy(src, dst, local_sem.at[n])
        for n, (src, dst) in enumerate(
            (
                (disp_hbm, ext_disp.at[own, :]),
                (pos_hbm, ext_pos.at[own, :]),
                (near_pairs_hbm, near_pairs),
                (basis_hbm, basis),
                (far_pairs_hbm, far_pairs),
                (intact_hbm, intact),
                (stiffness_hbm, stiffness),
                (far_hbm, far_blocks),
            )
        )
    ]
    for copy in loads:
        copy.start()
    barrier = pltpu.get_barrier_semaphore()
    peers = row_peers + col_peers + [next_id, last_id]
    for peer in peers:
        pl.semaphore_signal(barrier, inc=1, device_id=peer, device_id_type=MESH)

    for copy in loads[:3]:
        copy.wait()

    def lanes_of(c):
        return slice(c * ELEMS, (c + 1) * ELEMS)

    def thirds(x):
        high = x.astype(bf16).astype(f32)
        middle = (x - high).astype(bf16).astype(f32)
        return high, middle, (x - high) - middle

    def square_sum(x):
        return x[0] * x[0] + x[1] * x[1] + x[2] * x[2]

    gap = jnp.zeros((GROUPS, LANES - ELEMS), f32)
    one = jnp.ones((GROUPS, LANES), f32)
    none = jnp.zeros((GROUPS, LANES), f32)

    def rows_of(n, stride):
        return pl.ds(n, GROUPS, stride=stride)

    def widen(n, ext, c, halo):
        wide[n, 2 : OWN + 2, 0:ELEMS] = ext[0:OWN, lanes_of(c)]
        if halo:
            wide[n, 0:2, 0:ELEMS] = ext[126:128, lanes_of(c)]
            wide[n, OWN + 2 : OWN + 4, 0:ELEMS] = ext[OWN : OWN + 2, lanes_of(c)]

    def build(halo):
        for c in range(3):
            widen(c, ext_pos, c, halo)
            widen(3 + c, ext_disp, c, halo)
        centre = []
        for c in range(3):
            inner = wide[c, rows_of(3, 4), :][:, :ELEMS] + wide[c, rows_of(4, 4), :][:, :ELEMS]
            centre.append(jnp.sum(inner, axis=1, keepdims=True) * (0.5 / ELEMS))
        if not halo:
            for m in range(4):
                x = [wide[c, rows_of(2 + m, 4), :][:, :ELEMS] - centre[c] for c in range(3)]
                x = [jnp.concatenate([v, gap], axis=1) for v in x]
                parts = [thirds(v) for v in x]
                norm = thirds(square_sum(x))
                for c in range(3):
                    centred[c, rows_of(m, 4), :] = x[c]
                    for n, (a, _) in enumerate(PIECES):
                        left[rows_of(24 * m + 3 * n + c, 96), :] = parts[c][a]
                for n in range(3):
                    left[rows_of(24 * m + 18 + n, 96), :] = one
                    left[rows_of(24 * m + 21 + n, 96), :] = norm[n]

        def packed(n, half):
            a0, a1, a2, a3 = [wide[n, rows_of(4 * half + m, 4), :][:, :ELEMS] for m in range(4)]
            return (
                jnp.concatenate([a0, a1[:, :32]], axis=1),
                jnp.concatenate([a1[:, 32:], a2[:, :64]], axis=1),
                jnp.concatenate([a2[:, 64:], a3], axis=1),
            )

        for half in range(2):
            sources = [packed(n, half) for n in range(6)]
            for v in range(3):
                w = 3 * half + v
                y = [sources[c][v] - centre[c] for c in range(3)]
                u = [sources[3 + c][v] for c in range(3)]
                y_parts = [thirds(value) for value in y]
                u_parts = [thirds(value) for value in u]
                norm = thirds(square_sum(y) + core_square)
                inner = thirds(y[0] * u[0] + y[1] * u[1] + y[2] * u[2])
                for c in range(3):
                    for n, (_, b) in enumerate(PIECES):
                        right_q[w, rows_of(3 * n + c, 24), :] = -2.0 * y_parts[c][b]
                        right_s[w, rows_of(3 * n + c, 24), :] = u_parts[c][b]
                    disp_rows[w, rows_of(c, 8), :] = u[c]
                    pos_rows[w, rows_of(c, 8), :] = 3.0 * y[c]
                for n in range(3):
                    right_q[w, rows_of(18 + n, 24), :] = norm[n]
                    right_s[w, rows_of(18 + n, 24), :] = -inner[n]
                    right_q[w, rows_of(21 + n, 24), :] = one
                    right_s[w, rows_of(21 + n, 24), :] = none
                for n in range(3, 8):
                    disp_rows[w, rows_of(n, 8), :] = none
                    pos_rows[w, rows_of(n, 8), :] = 3.0 * one if n == 3 else none

    wide[...] = jnp.zeros_like(wide)
    build(False)

    slots = near_pairs.shape[1]
    near_target = near_pairs[0:1, :]
    live = lax.broadcasted_iota(jnp.int32, (1, slots), 1) < near_count[0]
    place = near_pairs[1:2, :] - near_target // 4 * 4
    row_is = lax.broadcasted_iota(jnp.int32, (OWN, slots), 0) == jnp.where(live, near_target, -1)
    lane_is = lax.broadcasted_iota(jnp.int32, (8 * ELEMS, slots), 0) // ELEMS == place
    row_is = row_is.astype(f32).astype(bf16)
    for w in range(6):
        weights[w] = lax.dot_general(
            row_is,
            lane_is[w * LANES : (w + 1) * LANES].astype(f32).astype(bf16),
            (((1,), (1,)), ((), ())),
            preferred_element_type=f32,
        )

    def halves(x):
        high = x.astype(bf16)
        return high, (x - high.astype(f32)).astype(bf16)

    def three_rows(x):
        return jnp.concatenate(thirds(x) + (jnp.zeros_like(x),), axis=0).astype(bf16)

    def near_groups(first, last):
        def near_group(g, _):
            top = pl.multiple_of(g * 24, 8)
            right = [
                jnp.concatenate([right_q[w, pl.ds(top, 24), :], right_s[w, pl.ds(top, 24), :]], axis=1).astype(bf16)
                for w in range(6)
            ]
            eight = pl.ds(pl.multiple_of(g * 8, 8), 8)
            for m in range(4):
                mine = left[pl.ds(pl.multiple_of(g * 96 + 24 * m, 8), 24), :]
                mine = mine.T[:ELEMS].astype(bf16)
                total = jnp.zeros((ELEMS, 32), f32)
                for w in SEEN[m]:
                    both = jnp.dot(mine, right[w], preferred_element_type=f32)
                    inverse = lax.rsqrt(jnp.maximum(both[:, :LANES], core_square))
                    square = inverse * inverse
                    cube = square * inverse
                    pull = both[:, LANES:] * square * cube
                    values = jnp.concatenate(halves(cube) + halves(pull), axis=1)
                    count = jnp.broadcast_to(weights[w, pl.ds(4 * g + m, 1), :], (8, LANES))
                    u_rows = three_rows(disp_rows[w, eight, :] * count)
                    y_rows = three_rows(pos_rows[w, eight, :] * count)
                    total = total + lax.dot_general(
                        values,
                        jnp.concatenate([u_rows, u_rows, y_rows, y_rows], axis=1),
                        (((1,), (1,)), ((), ())),
                        preferred_element_type=f32,
                    )
                total = total.T
                total = total[0:8] + total[8:16] + total[16:24]
                for c in range(3):
                    row = pl.ds(4 * g + m, 1)
                    near_rows[c, row, 0:ELEMS] = total[c : c + 1] - centred[c, row, 0:ELEMS] * total[3:4]
            return 0

        lax.fori_loop(first, last, near_group, 0)

    loads[3].wait()

    def project(block, coeff):
        top = pl.multiple_of(block * 8, 8)
        rows = ext_disp[pl.ds(top, 8), :].astype(bf16).astype(f32)
        lane = lax.broadcasted_iota(jnp.int32, (RANK, OWN), 1)
        for n in range(8):
            product = basis[top + n].astype(f32) * rows[n : n + 1, :]
            coeff = jnp.where(lane == top + n, jnp.sum(product, axis=1, keepdims=True), coeff)
        return coeff

    coeff = lax.fori_loop(0, OWN // 8, project, jnp.zeros((RANK, OWN), f32))
    own_rows = pl.ds(pl.multiple_of(i * OWN, OWN), OWN)
    column[own_rows, :] = coeff.astype(bf16)

    near_groups(*FIRST)
    pl.semaphore_wait(barrier, len(peers))

    def remote(src, dst, send, recv, peer):
        return pltpu.make_async_remote_copy(
            src_ref=src, dst_ref=dst, send_sem=send, recv_sem=recv, device_id=peer, device_id_type=MESH
        )

    mine = column.at[own_rows, :]
    gathers = [
        remote(mine, mine, gather_send.at[d], gather_recv.at[d], peer) for d, peer in enumerate(row_peers)
    ]
    halos = []
    for n, (src, dst) in enumerate(((disp_hbm, ext_disp), (pos_hbm, ext_pos))):
        halos.append(remote(src.at[pl.ds(OWN - 8, 8), :], dst.at[pl.ds(120, 8), :], halo_send.at[n], halo_recv.at[n], next_id))
        halos.append(remote(src.at[pl.ds(0, 8), :], dst.at[pl.ds(OWN, 8), :], halo_send.at[2 + n], halo_recv.at[2 + n], last_id))
    for copy in gathers + halos:
        copy.start()

    near_groups(*SECOND)

    for copy in gathers:
        copy.wait()
    for copy in loads[4:]:
        copy.wait()
    column_turned = jnp.concatenate([column[n * OWN : (n + 1) * OWN, :] for n in range(n_rows)], axis=1)
    far_slots = far_pairs.shape[1]
    sources = n_rows * OWN

    def couple(block, _):
        first = pl.multiple_of(block * LANES, LANES)
        source = far_pairs[1:2, pl.ds(first, LANES)]
        alive = lax.broadcasted_iota(jnp.int32, (1, LANES), 1) + first < far_count[0]
        source = jnp.where(alive, source, -1)
        chosen = (lax.broadcasted_iota(jnp.int32, (sources, LANES), 0) == source).astype(f32).astype(bf16)
        gathered = jnp.dot(column_turned, chosen, preferred_element_type=f32)

        def ranks(part, _):
            top = pl.multiple_of(part * 8, 8)
            blocks = far_blocks[pl.ds(top, 8), :, pl.ds(first, LANES)].astype(f32)
            coupled[pl.ds(top, 8), pl.ds(first, LANES)] = jnp.sum(blocks * gathered[None], axis=1)
            return 0

        return lax.fori_loop(0, RANK // 8, ranks, 0)

    lax.fori_loop(0, far_slots // LANES, couple, 0)
    whole = coupled[...]
    high = whole.astype(bf16)
    split[0:RANK, :] = high
    split[RANK : 2 * RANK, :] = (whole - high.astype(f32)).astype(bf16)

    def collect(block, _):
        first = pl.multiple_of(block * LANES, LANES)
        chosen = (lax.broadcasted_iota(jnp.int32, (LANES, far_slots), 0) + first == far_pairs[0:1, :]).astype(f32)
        both = lax.dot_general(
            chosen.astype(bf16), split[...], (((1,), (1,)), ((), ())), preferred_element_type=f32
        )
        partial[pl.ds(first, LANES), :] = (both[:, :RANK] + both[:, RANK:]).astype(bf16)
        return 0

    lax.fori_loop(0, n_cols * OWN // LANES, collect, 0)

    for copy in halos:
        copy.wait()

    here = pl.ds(pl.multiple_of(j * OWN, OWN), OWN)
    scatters = []
    for d, peer in enumerate(col_peers):
        block = partial.at[pl.ds(pl.multiple_of(peer[1] * OWN, OWN), OWN), :]
        scatters.append(remote(block, arrived.at[here, :], scatter_send.at[d], scatter_recv.at[d], peer))
    for copy in scatters:
        copy.start()
    arrived[here, :] = partial[here, :]

    ext_disp[OWN : OWN + 8, :] = jnp.where(me == devices - 1, 0.0, ext_disp[OWN : OWN + 8, :])
    ext_disp[120:128, :] = jnp.where(me == 0, 0.0, ext_disp[120:128, :])
    build(True)
    near_groups(*THIRD)
    near_groups(0, 1)

    parts = [near_rows[c, :, 0:ELEMS] for c in range(3)]
    u = [ext_disp[0:OWN, lanes_of(c)] for c in range(3)]
    separation = jnp.sqrt(1.0 + (u[0] * u[0] + u[1] * u[1] + u[2] * u[2]))
    softened = 1.0 - jnp.exp(-(separation - 1.0) / softening)
    whole_element = intact[...].astype(f32)
    damage = whole_element * softened + (1.0 - whole_element)
    damage_out[...] = damage
    held = (1.0 - damage) * stiffness[...]
    base_out[...] = jnp.concatenate([parts[c] - held * u[c] for c in range(3)], axis=1)

    for copy in scatters:
        copy.wait()
    owned = arrived[0:OWN, :].astype(f32)
    for n in range(1, n_cols):
        owned = owned + arrived[n * OWN : (n + 1) * OWN, :].astype(f32)
    owned_out[...] = owned.astype(bf16)


def local(
    displacement,
    positions,
    cluster_basis,
    near_pairs,
    near_count,
    far_pairs,
    far_count,
    far_blocks,
    intact,
    stiffness,
):
    n_rows, n_cols = lax.axis_size("rows"), lax.axis_size("cols")
    f32, bf16 = jnp.float32, jnp.bfloat16
    far_slots = far_pairs.shape[0]
    vmem = pl.BlockSpec(memory_space=pltpu.VMEM)
    smem = pl.BlockSpec(memory_space=pltpu.SMEM)
    hbm = pl.BlockSpec(memory_space=pltpu.HBM)
    base, damage, owned = pl.pallas_call(
        functools.partial(mega, n_rows, n_cols),
        out_shape=(
            jax.ShapeDtypeStruct((OWN, WIDTH), f32),
            jax.ShapeDtypeStruct((OWN, ELEMS), f32),
            jax.ShapeDtypeStruct((OWN, RANK), bf16),
        ),
        in_specs=[smem, smem] + [hbm] * 8,
        out_specs=(vmem, vmem, vmem),
        scratch_shapes=[
            pltpu.VMEM((2 * OWN, WIDTH), f32),
            pltpu.VMEM((2 * OWN, WIDTH), f32),
            pltpu.VMEM((2, near_pairs.shape[0]), jnp.int32),
            pltpu.VMEM((2, far_slots), jnp.int32),
            pltpu.VMEM((OWN, ELEMS), jnp.int32),
            pltpu.VMEM((OWN, ELEMS), f32),
            pltpu.VMEM((6, OWN + 8, LANES), f32),
            pltpu.VMEM((3, OWN, LANES), f32),
            pltpu.VMEM((24 * OWN, LANES), f32),
            pltpu.VMEM((6, 24 * GROUPS, LANES), f32),
            pltpu.VMEM((6, 24 * GROUPS, LANES), f32),
            pltpu.VMEM((6, 8 * GROUPS, LANES), f32),
            pltpu.VMEM((6, 8 * GROUPS, LANES), f32),
            pltpu.VMEM((6, OWN, LANES), f32),
            pltpu.VMEM((3, OWN, LANES), f32),
            pltpu.VMEM((OWN, RANK, WIDTH), bf16),
            pltpu.VMEM((RANK, RANK, far_slots), bf16),
            pltpu.VMEM((n_rows * OWN, RANK), bf16),
            pltpu.VMEM((RANK, far_slots), f32),
            pltpu.VMEM((2 * RANK, far_slots), bf16),
            pltpu.VMEM((n_cols * OWN, RANK), bf16),
            pltpu.VMEM((n_cols * OWN, RANK), bf16),
            pltpu.SemaphoreType.DMA((8,)),
            pltpu.SemaphoreType.DMA((4,)),
            pltpu.SemaphoreType.DMA((4,)),
            pltpu.SemaphoreType.DMA((n_rows - 1,)),
            pltpu.SemaphoreType.DMA((n_rows - 1,)),
            pltpu.SemaphoreType.DMA((n_cols - 1,)),
            pltpu.SemaphoreType.DMA((n_cols - 1,)),
        ],
        compiler_params=pltpu.CompilerParams(
            collective_id=0, has_side_effects=True, vmem_limit_bytes=60 * 1024 * 1024
        ),
        name="traction",
    )(
        near_count,
        far_count,
        displacement,
        positions,
        near_pairs.T,
        far_pairs.T,
        intact,
        stiffness,
        jnp.transpose(cluster_basis, (0, 2, 1)),
        jnp.transpose(far_blocks, (1, 2, 0)),
    )
    far_part = jnp.einsum("kfr,kr->kf", cluster_basis, owned, preferred_element_type=f32)
    return (base + far_part, damage)


def solution(mesh):
    both = ("rows", "cols")
    in_specs = (
        P(both, None),
        P(both, None),
        P(both, None, None),
        P(both, None),
        P(both),
        P(both, None),
        P(both),
        P(both, None, None),
        P(both, None),
        P(both, None),
    )
    out_specs = (P(both, None), P(both, None))
    return jax.shard_map(local, mesh=mesh, in_specs=in_specs, out_specs=out_specs, check_vma=False)
```

```python
import functools

import jax
import jax.numpy as jnp
from jax import lax
from jax.experimental import pallas as pl
from jax.experimental.pallas import tpu as pltpu
from jax.sharding import PartitionSpec as P

LOGICAL = pl.DeviceIdType.LOGICAL
ELEMS = 96
RANK = 64
OWN = 64
WIDTH = 3 * ELEMS
LANES = 128
GROUPS = OWN // 4
core_square = 0.25
softening = 1.5

PIECES = ((0, 0), (0, 1), (1, 0), (1, 1), (0, 2), (2, 0))
SEEN = (range(0, 4), range(0, 5), range(1, 6), range(2, 6))
FIRST = (1, 6)
SECOND = (6, 11)
THIRD = (11, 16)


def mega(
    n_rows,
    n_cols,
    near_count,
    far_count,
    disp_hbm,
    pos_hbm,
    near_pairs_hbm,
    far_pairs_hbm,
    intact_hbm,
    stiffness_hbm,
    basis_hbm,
    far_hbm,
    net_out,
    damage_out,
    ext_disp,
    ext_pos,
    near_pairs,
    far_pairs,
    intact,
    stiffness,
    wide,
    centred,
    left,
    lefts,
    sums,
    right_q,
    right_s,
    disp_rows,
    pos_rows,
    weights,
    near_rows,
    basis,
    far_blocks,
    column,
    coupled,
    partial,
    arrived,
    local_sem,
    halo_send,
    halo_recv,
    gather_send,
    gather_recv,
    scatter_send,
    scatter_recv,
):
    f32, bf16 = jnp.float32, jnp.bfloat16
    i, j = lax.axis_index("rows"), lax.axis_index("cols")
    me = i * n_cols + j
    devices = n_rows * n_cols
    next_id = lax.rem(me + 1, devices)
    last_id = lax.rem(me + devices - 1, devices)
    row_peers = [lax.rem(me + d * n_cols, devices) for d in range(1, n_rows)]
    col_places = [lax.rem(j + d, n_cols) for d in range(1, n_cols)]
    col_peers = [i * n_cols + place for place in col_places]

    own = pl.ds(0, OWN)
    loads = [
        pltpu.make_async_copy(src, dst, local_sem.at[n])
        for n, (src, dst) in enumerate(
            (
                (disp_hbm, ext_disp.at[own, :]),
                (pos_hbm, ext_pos.at[own, :]),
                (near_pairs_hbm, near_pairs),
                (basis_hbm, basis),
                (far_pairs_hbm, far_pairs),
                (intact_hbm, intact),
                (stiffness_hbm, stiffness),
                (far_hbm, far_blocks),
            )
        )
    ]
    for copy in loads:
        copy.start()
    barrier = pltpu.get_barrier_semaphore()
    peers = row_peers + col_peers + [next_id, last_id]
    for peer in peers:
        pl.semaphore_signal(barrier, inc=1, device_id=peer, device_id_type=LOGICAL)

    for copy in loads[:3]:
        copy.wait()

    def lanes_of(c):
        return slice(c * ELEMS, (c + 1) * ELEMS)

    def thirds(x):
        high = x.astype(bf16).astype(f32)
        middle = (x - high).astype(bf16).astype(f32)
        return high, middle, (x - high) - middle

    def square_sum(x):
        return x[0] * x[0] + x[1] * x[1] + x[2] * x[2]

    gap = jnp.zeros((GROUPS, LANES - ELEMS), f32)
    one = jnp.ones((GROUPS, LANES), f32)
    none = jnp.zeros((GROUPS, LANES), f32)

    def rows_of(n, stride):
        return pl.ds(n, GROUPS, stride=stride)

    def block_of(n):
        return slice(GROUPS * n, GROUPS * (n + 1))

    def widen(n, ext, c, halo):
        wide[n, 2 : OWN + 2, 0:ELEMS] = ext[0:OWN, lanes_of(c)]
        if halo:
            wide[n, 0:2, 0:ELEMS] = ext[126:128, lanes_of(c)]
            wide[n, OWN + 2 : OWN + 4, 0:ELEMS] = ext[OWN : OWN + 2, lanes_of(c)]

    def build(halo):
        for c in range(3):
            widen(c, ext_pos, c, halo)
            widen(3 + c, ext_disp, c, halo)
        centre = []
        for c in range(3):
            inner = wide[c, rows_of(3, 4), :][:, :ELEMS] + wide[c, rows_of(4, 4), :][:, :ELEMS]
            centre.append(jnp.sum(inner, axis=1, keepdims=True) * (0.5 / ELEMS))
        if not halo:
            for m in range(4):
                x = [wide[c, rows_of(2 + m, 4), :][:, :ELEMS] - centre[c] for c in range(3)]
                x = [jnp.concatenate([v, gap], axis=1) for v in x]
                parts = [thirds(v) for v in x]
                norm = thirds(square_sum(x))
                for c in range(3):
                    centred[c, rows_of(m, 4), :] = x[c]
                    for n, (a, _) in enumerate(PIECES):
                        left[m, block_of(3 * n + c), :] = parts[c][a]
                for n in range(3):
                    left[m, block_of(18 + n), :] = one
                    left[m, block_of(21 + n), :] = norm[n]

        def packed(n, half):
            a0, a1, a2, a3 = [wide[n, rows_of(4 * half + m, 4), :][:, :ELEMS] for m in range(4)]
            return (
                jnp.concatenate([a0, a1[:, :32]], axis=1),
                jnp.concatenate([a1[:, 32:], a2[:, :64]], axis=1),
                jnp.concatenate([a2[:, 64:], a3], axis=1),
            )

        for half in range(2):
            sources = [packed(n, half) for n in range(6)]
            for v in range(3):
                if halo and v == 2 - 2 * half:
                    continue
                w = 3 * half + v
                y = [sources[c][v] - centre[c] for c in range(3)]
                u = [sources[3 + c][v] for c in range(3)]
                y_parts = [thirds(value) for value in y]
                u_parts = [thirds(value) for value in u]
                norm = thirds(square_sum(y) + core_square)
                inner = thirds(y[0] * u[0] + y[1] * u[1] + y[2] * u[2])
                for c in range(3):
                    for n, (_, b) in enumerate(PIECES):
                        right_q[w, block_of(3 * n + c), :] = -2.0 * y_parts[c][b]
                        right_s[w, block_of(3 * n + c), :] = u_parts[c][b]
                    disp_rows[w, block_of(c), :] = u[c]
                    pos_rows[w, block_of(c), :] = 3.0 * y[c]
                for n in range(3):
                    right_q[w, block_of(18 + n), :] = norm[n]
                    right_s[w, block_of(18 + n), :] = -inner[n]
                    right_q[w, block_of(21 + n), :] = one
                    right_s[w, block_of(21 + n), :] = none
                for n in range(3, 8):
                    disp_rows[w, block_of(n), :] = none
                    pos_rows[w, block_of(n), :] = 3.0 * one if n == 3 else none

    wide[...] = jnp.zeros_like(wide)
    build(False)

    slots = near_pairs.shape[1]
    near_target = near_pairs[0:1, :]
    live = lax.broadcasted_iota(jnp.int32, (1, slots), 1) < near_count[0]
    place = near_pairs[1:2, :] - near_target // 4 * 4
    row_is = lax.broadcasted_iota(jnp.int32, (OWN, slots), 0) == jnp.where(live, near_target, -1)
    lane_is = lax.broadcasted_iota(jnp.int32, (8 * ELEMS, slots), 0) // ELEMS == place
    row_is = row_is.astype(f32).astype(bf16)
    for w in range(6):
        weights[w] = lax.dot_general(
            row_is,
            lane_is[w * LANES : (w + 1) * LANES].astype(f32).astype(bf16),
            (((1,), (1,)), ((), ())),
            preferred_element_type=f32,
        )

    def halves(x):
        high = x.astype(bf16)
        return high, (x - high.astype(f32)).astype(bf16)

    def three_rows(x):
        return jnp.concatenate(thirds(x) + (jnp.zeros_like(x),), axis=0).astype(bf16)

    def turn(g, _):
        group = pl.ds(g, 24, stride=GROUPS)
        for m in range(4):
            lefts[4 * g + m] = left[m, group, :].T[:ELEMS].astype(bf16)
        return 0

    lax.fori_loop(0, GROUPS, turn, 0)

    def near_groups(first, last):
        def near_group(g, _):
            group = pl.ds(g, 24, stride=GROUPS)
            eight = pl.ds(g, 8, stride=GROUPS)
            rights, rows = [], []
            for w in range(6):
                rights.append(jnp.concatenate([right_q[w, group, :], right_s[w, group, :]], axis=1).astype(bf16))
                u_rows = three_rows(disp_rows[w, eight, :])
                y_rows = three_rows(pos_rows[w, eight, :])
                rows.append(jnp.concatenate([u_rows, u_rows, y_rows, y_rows], axis=1))
            totals = [None] * 4
            for n in range(5):
                for pair in range(2):
                    w = n + pair
                    seen = [m for m in (2 * pair, 2 * pair + 1) if w in SEEN[m]]
                    mine = jnp.concatenate([lefts[4 * g + m] for m in seen], axis=0)
                    both = jnp.dot(mine, rights[w], preferred_element_type=f32)
                    values = []
                    for at, m in enumerate(seen):
                        part = both[at * ELEMS : (at + 1) * ELEMS]
                        inverse = lax.rsqrt(jnp.maximum(part[:, :LANES], core_square))
                        square = inverse * inverse
                        cube = square * (inverse * weights[w, pl.ds(4 * g + m, 1), :])
                        pull = (part[:, LANES:] * square) * cube
                        values.append(jnp.concatenate(halves(cube) + halves(pull), axis=1))
                    added = lax.dot_general(
                        jnp.concatenate(values, axis=0), rows[w], (((1,), (1,)), ((), ())), preferred_element_type=f32
                    )
                    for at, m in enumerate(seen):
                        piece = added[at * ELEMS : (at + 1) * ELEMS]
                        totals[m] = piece if totals[m] is None else totals[m] + piece
            for m in range(4):
                sums[4 * g + m] = totals[m]
            return 0

        lax.fori_loop(first, last, near_group, 0)

    loads[3].wait()

    def project(block, coeff):
        top = pl.multiple_of(block * 8, 8)
        rows = ext_disp[pl.ds(top, 8), :].astype(bf16)
        lane = lax.broadcasted_iota(jnp.int32, (RANK, OWN), 1)
        for n in range(8):
            product = basis[top + n] * rows[n : n + 1, :]
            product = product[:, :LANES].astype(f32) + product[:, LANES : 2 * LANES].astype(f32) + jnp.concatenate(
                [product[:, 2 * LANES :].astype(f32), jnp.zeros((RANK, 3 * LANES - WIDTH), f32)], axis=1
            )
            coeff = jnp.where(lane == top + n, jnp.sum(product, axis=1, keepdims=True), coeff)
        return coeff

    coeff = lax.fori_loop(0, OWN // 8, project, jnp.zeros((RANK, OWN), f32))
    own_rows = pl.ds(pl.multiple_of(i * OWN, OWN), OWN)
    column[own_rows, :] = coeff.astype(bf16)

    near_groups(*FIRST)
    pl.semaphore_wait(barrier, len(peers))

    def remote(src, dst, send, recv, peer):
        return pltpu.make_async_remote_copy(
            src_ref=src, dst_ref=dst, send_sem=send, recv_sem=recv, device_id=peer, device_id_type=LOGICAL
        )

    mine = column.at[own_rows, :]
    gathers = [
        remote(mine, mine, gather_send.at[d], gather_recv.at[d], peer) for d, peer in enumerate(row_peers)
    ]
    halos = []
    for n, (src, dst) in enumerate(((disp_hbm, ext_disp), (pos_hbm, ext_pos))):
        halos.append(remote(src.at[pl.ds(OWN - 8, 8), :], dst.at[pl.ds(120, 8), :], halo_send.at[n], halo_recv.at[n], next_id))
        halos.append(remote(src.at[pl.ds(0, 8), :], dst.at[pl.ds(OWN, 8), :], halo_send.at[2 + n], halo_recv.at[2 + n], last_id))
    for copy in gathers + halos:
        copy.start()

    near_groups(*SECOND)

    for copy in gathers:
        copy.wait()
    for copy in loads[4:]:
        copy.wait()
    column_turned = jnp.concatenate([column[n * OWN : (n + 1) * OWN, :] for n in range(n_rows)], axis=1)
    far_slots = far_pairs.shape[1]
    sources = n_rows * OWN

    wide_block = 2 * LANES
    fold = lax.broadcasted_iota(jnp.int32, (16, 256), 0) == lax.broadcasted_iota(jnp.int32, (16, 256), 1) // 16
    fold = fold.astype(f32).astype(bf16)

    def couple(block, _):
        first = pl.multiple_of(block * wide_block, wide_block)
        source = far_pairs[1:2, pl.ds(first, wide_block)]
        alive = lax.broadcasted_iota(jnp.int32, (1, wide_block), 1) + first < far_count[0]
        source = jnp.where(alive, source, -1)
        chosen = (lax.broadcasted_iota(jnp.int32, (sources, wide_block), 0) == source).astype(f32).astype(bf16)
        gathered = jnp.dot(column_turned, chosen, preferred_element_type=f32).astype(bf16)

        def ranks(part, _):
            top = pl.multiple_of(part * 16, 16)
            summed = []
            for n in range(16):
                product = far_blocks[top + n, :, pl.ds(first, wide_block)] * gathered
                summed.append((product[0:16] + product[16:32]) + (product[32:48] + product[48:64]))
            whole = jnp.dot(fold, jnp.concatenate(summed, axis=0), preferred_element_type=f32)
            coupled[pl.ds(top, 16), pl.ds(first, wide_block)] = whole.astype(bf16)
            return 0

        return lax.fori_loop(0, RANK // 16, ranks, 0)

    lax.fori_loop(0, far_slots // wide_block, couple, 0)

    def collect(block, _):
        first = pl.multiple_of(block * LANES, LANES)
        chosen = (lax.broadcasted_iota(jnp.int32, (LANES, far_slots), 0) + first == far_pairs[0:1, :]).astype(f32)
        partial[pl.ds(first, LANES), :] = lax.dot_general(
            chosen.astype(bf16), coupled[...], (((1,), (1,)), ((), ())), preferred_element_type=f32
        ).astype(bf16)
        return 0

    lax.fori_loop(0, n_cols * OWN // LANES, collect, 0)

    for copy in halos:
        copy.wait()

    here = pl.ds(pl.multiple_of(j * OWN, OWN), OWN)
    scatters = []
    for d, peer in enumerate(col_peers):
        block = partial.at[pl.ds(pl.multiple_of(col_places[d] * OWN, OWN), OWN), :]
        scatters.append(remote(block, arrived.at[here, :], scatter_send.at[d], scatter_recv.at[d], peer))
    for copy in scatters:
        copy.start()
    arrived[here, :] = partial[here, :]

    ext_disp[OWN : OWN + 8, :] = jnp.where(me == devices - 1, 0.0, ext_disp[OWN : OWN + 8, :])
    ext_disp[120:128, :] = jnp.where(me == 0, 0.0, ext_disp[120:128, :])
    build(True)
    near_groups(*THIRD)
    near_groups(0, 1)

    def settle(block, _):
        for n in range(4):
            row = pl.ds(4 * block + n, 1)
            total = sums[4 * block + n].T
            total = total[0:8] + total[8:16] + total[16:24]
            for c in range(3):
                near_rows[c, row, 0:ELEMS] = total[c : c + 1] - centred[c, row, 0:ELEMS] * total[3:4]
        return 0

    lax.fori_loop(0, OWN // 4, settle, 0)
    parts = [near_rows[c, :, 0:ELEMS] for c in range(3)]
    u = [ext_disp[0:OWN, lanes_of(c)] for c in range(3)]
    separation = jnp.sqrt(1.0 + (u[0] * u[0] + u[1] * u[1] + u[2] * u[2]))
    softened = 1.0 - jnp.exp(-(separation - 1.0) / softening)
    whole_element = intact[...].astype(f32)
    damage = whole_element * softened + (1.0 - whole_element)
    damage_out[...] = damage
    held = (1.0 - damage) * stiffness[...]
    base = jnp.concatenate([parts[c] - held * u[c] for c in range(3)], axis=1)

    for copy in scatters:
        copy.wait()
    owned = arrived[0:OWN, :].astype(f32)
    for n in range(1, n_cols):
        owned = owned + arrived[n * OWN : (n + 1) * OWN, :].astype(f32)
    owned = owned.T
    for block in range(OWN // 16):
        summed = []
        for n in range(16):
            k = 16 * block + n
            product = basis[k] * owned[:, k : k + 1].astype(bf16)
            summed.append((product[0:16] + product[16:32]) + (product[32:48] + product[48:64]))
        far = jnp.dot(fold, jnp.concatenate(summed, axis=0), preferred_element_type=f32)
        net_out[16 * block : 16 * block + 16, :] = base[16 * block : 16 * block + 16] + far


def local(
    displacement,
    positions,
    cluster_basis,
    near_pairs,
    near_count,
    far_pairs,
    far_count,
    far_blocks,
    intact,
    stiffness,
):
    n_rows, n_cols = lax.axis_size("rows"), lax.axis_size("cols")
    f32, bf16 = jnp.float32, jnp.bfloat16
    far_slots = far_pairs.shape[0]
    vmem = pl.BlockSpec(memory_space=pltpu.VMEM)
    smem = pl.BlockSpec(memory_space=pltpu.SMEM)
    hbm = pl.BlockSpec(memory_space=pltpu.HBM)
    return pl.pallas_call(
        functools.partial(mega, n_rows, n_cols),
        out_shape=(
            jax.ShapeDtypeStruct((OWN, WIDTH), f32),
            jax.ShapeDtypeStruct((OWN, ELEMS), f32),
        ),
        in_specs=[smem, smem] + [hbm] * 8,
        out_specs=(vmem, vmem),
        scratch_shapes=[
            pltpu.VMEM((2 * OWN, WIDTH), f32),
            pltpu.VMEM((2 * OWN, WIDTH), f32),
            pltpu.VMEM((2, near_pairs.shape[0]), jnp.int32),
            pltpu.VMEM((2, far_slots), jnp.int32),
            pltpu.VMEM((OWN, ELEMS), jnp.int32),
            pltpu.VMEM((OWN, ELEMS), f32),
            pltpu.VMEM((6, OWN + 8, LANES), f32),
            pltpu.VMEM((3, OWN, LANES), f32),
            pltpu.VMEM((4, 24 * GROUPS, LANES), f32),
            pltpu.VMEM((OWN, ELEMS, 24), bf16),
            pltpu.VMEM((OWN, ELEMS, 32), f32),
            pltpu.VMEM((6, 24 * GROUPS, LANES), f32),
            pltpu.VMEM((6, 24 * GROUPS, LANES), f32),
            pltpu.VMEM((6, 8 * GROUPS, LANES), f32),
            pltpu.VMEM((6, 8 * GROUPS, LANES), f32),
            pltpu.VMEM((6, OWN, LANES), f32),
            pltpu.VMEM((3, OWN, LANES), f32),
            pltpu.VMEM((OWN, RANK, WIDTH), bf16),
            pltpu.VMEM((RANK, RANK, far_slots), bf16),
            pltpu.VMEM((n_rows * OWN, RANK), bf16),
            pltpu.VMEM((RANK, far_slots), bf16),
            pltpu.VMEM((n_cols * OWN, RANK), bf16),
            pltpu.VMEM((n_cols * OWN, RANK), bf16),
            pltpu.SemaphoreType.DMA((8,)),
            pltpu.SemaphoreType.DMA((4,)),
            pltpu.SemaphoreType.DMA((4,)),
            pltpu.SemaphoreType.DMA((n_rows - 1,)),
            pltpu.SemaphoreType.DMA((n_rows - 1,)),
            pltpu.SemaphoreType.DMA((n_cols - 1,)),
            pltpu.SemaphoreType.DMA((n_cols - 1,)),
        ],
        compiler_params=pltpu.CompilerParams(
            collective_id=0, has_side_effects=True, vmem_limit_bytes=60 * 1024 * 1024
        ),
        name="traction",
    )(
        near_count,
        far_count,
        displacement,
        positions,
        near_pairs.T,
        far_pairs.T,
        intact,
        stiffness,
        jnp.transpose(cluster_basis, (0, 2, 1)),
        jnp.transpose(far_blocks, (1, 2, 0)),
    )


def solution(mesh):
    both = ("rows", "cols")
    in_specs = (
        P(both, None),
        P(both, None),
        P(both, None, None),
        P(both, None),
        P(both),
        P(both, None),
        P(both),
        P(both, None, None),
        P(both, None),
        P(both, None),
    )
    out_specs = (P(both, None), P(both, None))
    return jax.shard_map(local, mesh=mesh, in_specs=in_specs, out_specs=out_specs, check_vma=False)
```

```python
import functools

import jax
import jax.numpy as jnp
from jax import lax
from jax.experimental import pallas as pl
from jax.experimental.pallas import tpu as pltpu
from jax.sharding import PartitionSpec as P

LOGICAL = pl.DeviceIdType.LOGICAL
ELEMS = 96
RANK = 64
OWN = 64
WIDTH = 3 * ELEMS
LANES = 128
GROUPS = OWN // 4
core_square = 0.25
softening = 1.5

PIECES = ((0, 0), (0, 1), (1, 0), (1, 1), (0, 2), (2, 0))
SEEN = (range(0, 4), range(0, 5), range(1, 6), range(2, 6))
FIRST = (1, 7)
SECOND = (7, 11)
THIRD = (11, 16)


def mega(
    n_rows,
    n_cols,
    near_count,
    far_count,
    disp_hbm,
    pos_hbm,
    near_pairs_hbm,
    far_pairs_hbm,
    intact_hbm,
    stiffness_hbm,
    basis_hbm,
    far_hbm,
    net_out,
    damage_out,
    ext_disp,
    ext_pos,
    near_pairs,
    far_pairs,
    intact,
    stiffness,
    wide,
    centred,
    left,
    lefts,
    sums,
    right_q,
    right_s,
    disp_rows,
    pos_rows,
    weights,
    near_rows,
    basis,
    far_blocks,
    column,
    coupled,
    partial,
    arrived,
    local_sem,
    halo_send,
    halo_recv,
    gather_send,
    gather_recv,
    scatter_send,
    scatter_recv,
):
    f32, bf16 = jnp.float32, jnp.bfloat16
    i, j = lax.axis_index("rows"), lax.axis_index("cols")
    me = i * n_cols + j
    devices = n_rows * n_cols
    next_id = lax.rem(me + 1, devices)
    last_id = lax.rem(me + devices - 1, devices)
    row_peers = [lax.rem(me + d * n_cols, devices) for d in range(1, n_rows)]
    col_places = [lax.rem(j + d, n_cols) for d in range(1, n_cols)]
    col_peers = [i * n_cols + place for place in col_places]

    own = pl.ds(0, OWN)
    loads = [
        pltpu.make_async_copy(src, dst, local_sem.at[n])
        for n, (src, dst) in enumerate(
            (
                (disp_hbm, ext_disp.at[own, :]),
                (pos_hbm, ext_pos.at[own, :]),
                (near_pairs_hbm, near_pairs),
                (basis_hbm, basis),
                (far_pairs_hbm, far_pairs),
                (intact_hbm, intact),
                (stiffness_hbm, stiffness),
                (far_hbm, far_blocks),
            )
        )
    ]
    for copy in loads:
        copy.start()
    barrier = pltpu.get_barrier_semaphore()
    peers = row_peers + col_peers + [next_id, last_id]
    for peer in peers:
        pl.semaphore_signal(barrier, inc=1, device_id=peer, device_id_type=LOGICAL)

    for copy in loads[:3]:
        copy.wait()

    def lanes_of(c):
        return slice(c * ELEMS, (c + 1) * ELEMS)

    def thirds(x):
        high = x.astype(bf16).astype(f32)
        middle = (x - high).astype(bf16).astype(f32)
        return high, middle, (x - high) - middle

    def square_sum(x):
        return x[0] * x[0] + x[1] * x[1] + x[2] * x[2]

    gap = jnp.zeros((GROUPS, LANES - ELEMS), f32)
    one = jnp.ones((GROUPS, LANES), f32)
    none = jnp.zeros((GROUPS, LANES), f32)

    def rows_of(n, stride):
        return pl.ds(n, GROUPS, stride=stride)

    def block_of(n):
        return slice(GROUPS * n, GROUPS * (n + 1))

    def widen(n, ext, c, halo):
        wide[n, 2 : OWN + 2, 0:ELEMS] = ext[0:OWN, lanes_of(c)]
        if halo:
            wide[n, 0:2, 0:ELEMS] = ext[126:128, lanes_of(c)]
            wide[n, OWN + 2 : OWN + 4, 0:ELEMS] = ext[OWN : OWN + 2, lanes_of(c)]

    def build(halo):
        for c in range(3):
            widen(c, ext_pos, c, halo)
            widen(3 + c, ext_disp, c, halo)
        centre = []
        for c in range(3):
            inner = wide[c, rows_of(3, 4), :][:, :ELEMS] + wide[c, rows_of(4, 4), :][:, :ELEMS]
            centre.append(jnp.sum(inner, axis=1, keepdims=True) * (0.5 / ELEMS))
        if not halo:
            for m in range(4):
                x = [wide[c, rows_of(2 + m, 4), :][:, :ELEMS] - centre[c] for c in range(3)]
                x = [jnp.concatenate([v, gap], axis=1) for v in x]
                parts = [thirds(v) for v in x]
                norm = thirds(square_sum(x))
                for c in range(3):
                    centred[c, rows_of(m, 4), :] = x[c]
                    for n, (a, _) in enumerate(PIECES):
                        left[m, block_of(3 * n + c), :] = parts[c][a]
                for n in range(3):
                    left[m, block_of(18 + n), :] = one
                    left[m, block_of(21 + n), :] = norm[n]

        def packed(n, half):
            a0, a1, a2, a3 = [wide[n, rows_of(4 * half + m, 4), :][:, :ELEMS] for m in range(4)]
            return (
                jnp.concatenate([a0, a1[:, :32]], axis=1),
                jnp.concatenate([a1[:, 32:], a2[:, :64]], axis=1),
                jnp.concatenate([a2[:, 64:], a3], axis=1),
            )

        for half in range(2):
            sources = [packed(n, half) for n in range(6)]
            for v in range(3):
                if halo and v == 2 - 2 * half:
                    continue
                w = 3 * half + v
                y = [sources[c][v] - centre[c] for c in range(3)]
                u = [sources[3 + c][v] for c in range(3)]
                y_parts = [thirds(value) for value in y]
                u_parts = [thirds(value) for value in u]
                norm = thirds(square_sum(y) + core_square)
                inner = thirds(y[0] * u[0] + y[1] * u[1] + y[2] * u[2])
                for c in range(3):
                    for n, (_, b) in enumerate(PIECES):
                        right_q[w, block_of(3 * n + c), :] = -2.0 * y_parts[c][b]
                        right_s[w, block_of(3 * n + c), :] = u_parts[c][b]
                    triple = thirds(3.0 * y[c])
                    for n in range(2):
                        disp_rows[w, block_of(4 * n + c), :] = u_parts[c][n]
                        pos_rows[w, block_of(4 * n + c), :] = triple[n]
                for n in range(3):
                    right_q[w, block_of(18 + n), :] = norm[n]
                    right_s[w, block_of(18 + n), :] = -inner[n]
                    right_q[w, block_of(21 + n), :] = one
                    right_s[w, block_of(21 + n), :] = none
                for n in (3, 7):
                    disp_rows[w, block_of(n), :] = none
                    pos_rows[w, block_of(n), :] = 3.0 * one if n == 3 else none

    wide[...] = jnp.zeros_like(wide)
    build(False)

    slots = near_pairs.shape[1]
    near_target = near_pairs[0:1, :]
    live = lax.broadcasted_iota(jnp.int32, (1, slots), 1) < near_count[0]
    place = near_pairs[1:2, :] - near_target // 4 * 4
    row_is = lax.broadcasted_iota(jnp.int32, (OWN, slots), 0) == jnp.where(live, near_target, -1)
    lane_is = lax.broadcasted_iota(jnp.int32, (8 * ELEMS, slots), 0) // ELEMS == place
    row_is = row_is.astype(f32).astype(bf16)
    for w in range(6):
        weights[w] = lax.dot_general(
            row_is,
            lane_is[w * LANES : (w + 1) * LANES].astype(f32).astype(bf16),
            (((1,), (1,)), ((), ())),
            preferred_element_type=f32,
        )

    def halves(x):
        high = x.astype(bf16)
        return high, (x - high.astype(f32)).astype(bf16)

    def turn(g):
        for m in range(4):
            lefts[4 * g + m] = left[m, pl.ds(g, 24, stride=GROUPS), :].T[:ELEMS].astype(bf16)

    def settle(g):
        for m in range(4):
            row = pl.ds(4 * g + m, 1)
            total = sums[4 * g + m].T
            total = total[0:4] + total[4:8]
            for c in range(3):
                near_rows[c, row, 0:ELEMS] = total[c : c + 1] - centred[c, row, 0:ELEMS] * total[3:4]

    turn(0)
    turn(1)

    def near_groups(first, last):
        def near_group(g, _):
            group = pl.ds(g, 24, stride=GROUPS)
            eight = pl.ds(g, 8, stride=GROUPS)
            rows, boths = [], []
            for w in range(6):
                right = jnp.concatenate([right_q[w, group, :], right_s[w, group, :]], axis=1).astype(bf16)
                u_rows = disp_rows[w, eight, :].astype(bf16)
                y_rows = pos_rows[w, eight, :].astype(bf16)
                rows.append(jnp.concatenate([u_rows, u_rows, y_rows, y_rows], axis=1))
                seen = [m for m in range(4) if w in SEEN[m]]
                mine = jnp.concatenate([lefts[4 * g + m] for m in seen], axis=0)
                both = jnp.dot(mine, right, preferred_element_type=f32)
                boths.append({m: both[at * ELEMS : (at + 1) * ELEMS] for at, m in enumerate(seen)})
            totals = [None] * 4
            for n in range(5):
                for pair in range(2):
                    w = n + pair
                    seen = [m for m in (2 * pair, 2 * pair + 1) if w in SEEN[m]]
                    values = []
                    for m in seen:
                        part = boths[w][m]
                        inverse = lax.rsqrt(jnp.maximum(part[:, :LANES], core_square))
                        square = inverse * inverse
                        cube = square * (inverse * weights[w, pl.ds(4 * g + m, 1), :])
                        pull = (part[:, LANES:] * square) * cube
                        values.append(jnp.concatenate(halves(cube) + halves(pull), axis=1))
                    added = lax.dot_general(
                        jnp.concatenate(values, axis=0), rows[w], (((1,), (1,)), ((), ())), preferred_element_type=f32
                    )
                    for at, m in enumerate(seen):
                        piece = added[at * ELEMS : (at + 1) * ELEMS]
                        totals[m] = piece if totals[m] is None else totals[m] + piece
            settle(jnp.maximum(g - 1, 0))
            for m in range(4):
                sums[4 * g + m] = totals[m]
            turn(jnp.minimum(g + 1, GROUPS - 1))
            return 0

        lax.fori_loop(first, last, near_group, 0)
        settle(last - 1)

    loads[3].wait()

    def project(block, coeff):
        top = pl.multiple_of(block * 8, 8)
        rows = ext_disp[pl.ds(top, 8), :].astype(bf16)
        lane = lax.broadcasted_iota(jnp.int32, (RANK, OWN), 1)
        for n in range(8):
            product = basis[top + n] * rows[n : n + 1, :]
            product = product[:, :LANES].astype(f32) + product[:, LANES : 2 * LANES].astype(f32) + jnp.concatenate(
                [product[:, 2 * LANES :].astype(f32), jnp.zeros((RANK, 3 * LANES - WIDTH), f32)], axis=1
            )
            coeff = jnp.where(lane == top + n, jnp.sum(product, axis=1, keepdims=True), coeff)
        return coeff

    coeff = lax.fori_loop(0, OWN // 8, project, jnp.zeros((RANK, OWN), f32))
    half = OWN // 2

    def pack(block):
        return jnp.concatenate([block[:half], block[half:]], axis=1).astype(bf16)

    own_rows = pl.ds(pl.multiple_of(i * half, half), half)
    column[own_rows, :] = pack(coeff)

    near_groups(*FIRST)
    pl.semaphore_wait(barrier, len(peers))

    def remote(src, dst, send, recv, peer):
        return pltpu.make_async_remote_copy(
            src_ref=src, dst_ref=dst, send_sem=send, recv_sem=recv, device_id=peer, device_id_type=LOGICAL
        )

    mine = column.at[own_rows, :]
    gathers = [
        remote(mine, mine, gather_send.at[d], gather_recv.at[d], peer) for d, peer in enumerate(row_peers)
    ]
    halos = []
    for n, (src, dst) in enumerate(((disp_hbm, ext_disp), (pos_hbm, ext_pos))):
        halos.append(remote(src.at[pl.ds(OWN - 8, 8), :], dst.at[pl.ds(120, 8), :], halo_send.at[n], halo_recv.at[n], next_id))
        halos.append(remote(src.at[pl.ds(0, 8), :], dst.at[pl.ds(OWN, 8), :], halo_send.at[2 + n], halo_recv.at[2 + n], last_id))
    for copy in gathers + halos:
        copy.start()

    near_groups(*SECOND)

    for copy in gathers:
        copy.wait()
    for copy in loads[4:]:
        copy.wait()
    tops = [column[n * half : (n + 1) * half, :RANK] for n in range(n_rows)]
    bottoms = [column[n * half : (n + 1) * half, RANK:] for n in range(n_rows)]
    column_turned = jnp.concatenate(
        [jnp.concatenate(tops, axis=1), jnp.concatenate(bottoms, axis=1)], axis=0
    )
    far_slots = far_pairs.shape[1]
    sources = n_rows * OWN

    wide_block = 2 * LANES
    sublane = lax.broadcasted_iota(jnp.int32, (8, wide_block), 0)

    def merge(blocks):
        reach = 4
        while len(blocks) > 1:
            upper = sublane // reach % 2 == 0
            count = len(blocks) // 2
            pairs = [(blocks[n], blocks[n + count]) for n in range(count)]
            blocks = []
            for x, y in pairs:
                crossed = jnp.where(upper, y, x)
                moved = pltpu.roll(crossed, reach, axis=0)
                if reach < 4:
                    moved = jnp.where(upper, pltpu.roll(crossed, 8 - reach, axis=0), moved)
                blocks.append(jnp.where(upper, x, y) + moved)
            reach //= 2
        return blocks[0]

    def couple(block, _):
        first = pl.multiple_of(block * wide_block, wide_block)
        source = far_pairs[1:2, pl.ds(first, wide_block)]
        alive = lax.broadcasted_iota(jnp.int32, (1, wide_block), 1) + first < far_count[0]
        source = jnp.where(alive, source, -1)
        chosen = (lax.broadcasted_iota(jnp.int32, (sources, wide_block), 0) == source).astype(f32).astype(bf16)
        gathered = jnp.dot(column_turned, chosen, preferred_element_type=f32).astype(bf16)

        def ranks(part, _):
            top = pl.multiple_of(part * 16, 16)
            summed = []
            for n in range(16):
                product = far_blocks[top + n, :, pl.ds(first, wide_block)] * gathered
                product = ((product[0:16] + product[16:32]) + (product[32:48] + product[48:64])).astype(f32)
                summed.append(product[0:8] + product[8:16])
            whole = jnp.concatenate([merge(summed[:8]), merge(summed[8:])], axis=0)
            coupled[pl.ds(top, 16), pl.ds(first, wide_block)] = whole.astype(bf16)
            return 0

        return lax.fori_loop(0, RANK // 16, ranks, 0)

    lax.fori_loop(0, far_slots // wide_block, couple, 0)

    def collect(block, _):
        first = pl.multiple_of(block * wide_block, wide_block)
        chosen = lax.broadcasted_iota(jnp.int32, (wide_block, far_slots), 0) + first == far_pairs[0:1, :]
        found = lax.dot_general(
            chosen.astype(f32).astype(bf16), coupled[...], (((1,), (1,)), ((), ())), preferred_element_type=f32
        )
        for n in range(wide_block // OWN):
            to = pl.multiple_of(block * (wide_block // 2) + n * half, half)
            partial[pl.ds(to, half), :] = pack(found[n * OWN : (n + 1) * OWN])
        return 0

    lax.fori_loop(0, n_cols * OWN // wide_block, collect, 0)

    for copy in halos:
        copy.wait()

    here = pl.ds(pl.multiple_of(j * half, half), half)
    scatters = []
    for d, peer in enumerate(col_peers):
        block = partial.at[pl.ds(pl.multiple_of(col_places[d] * half, half), half), :]
        scatters.append(remote(block, arrived.at[here, :], scatter_send.at[d], scatter_recv.at[d], peer))
    for copy in scatters:
        copy.start()
    arrived[here, :] = partial[here, :]

    ext_disp[OWN : OWN + 8, :] = jnp.where(me == devices - 1, 0.0, ext_disp[OWN : OWN + 8, :])
    ext_disp[120:128, :] = jnp.where(me == 0, 0.0, ext_disp[120:128, :])
    build(True)
    near_groups(*THIRD)
    near_groups(0, 1)

    parts = [near_rows[c, :, 0:ELEMS] for c in range(3)]
    u = [ext_disp[0:OWN, lanes_of(c)] for c in range(3)]
    separation = jnp.sqrt(1.0 + (u[0] * u[0] + u[1] * u[1] + u[2] * u[2]))
    softened = 1.0 - jnp.exp(-(separation - 1.0) / softening)
    whole_element = intact[...].astype(f32)
    damage = whole_element * softened + (1.0 - whole_element)
    damage_out[...] = damage
    held = (1.0 - damage) * stiffness[...]
    base = jnp.concatenate([parts[c] - held * u[c] for c in range(3)], axis=1)

    for copy in scatters:
        copy.wait()
    owned = arrived[0:half, :].astype(f32)
    for n in range(1, n_cols):
        owned = owned + arrived[n * half : (n + 1) * half, :].astype(f32)
    owned = owned.T
    owned = jnp.concatenate([owned[:RANK], owned[RANK:]], axis=1)
    fold = lax.broadcasted_iota(jnp.int32, (16, 256), 0) == lax.broadcasted_iota(jnp.int32, (16, 256), 1) // 16
    fold = fold.astype(f32).astype(bf16)
    for block in range(OWN // 16):
        summed = []
        for n in range(16):
            k = 16 * block + n
            product = basis[k] * owned[:, k : k + 1].astype(bf16)
            summed.append((product[0:16] + product[16:32]) + (product[32:48] + product[48:64]))
        far = jnp.dot(fold, jnp.concatenate(summed, axis=0), preferred_element_type=f32)
        net_out[16 * block : 16 * block + 16, :] = base[16 * block : 16 * block + 16] + far


def local(
    displacement,
    positions,
    cluster_basis,
    near_pairs,
    near_count,
    far_pairs,
    far_count,
    far_blocks,
    intact,
    stiffness,
):
    n_rows, n_cols = lax.axis_size("rows"), lax.axis_size("cols")
    f32, bf16 = jnp.float32, jnp.bfloat16
    far_slots = far_pairs.shape[0]
    vmem = pl.BlockSpec(memory_space=pltpu.VMEM)
    smem = pl.BlockSpec(memory_space=pltpu.SMEM)
    hbm = pl.BlockSpec(memory_space=pltpu.HBM)
    return pl.pallas_call(
        functools.partial(mega, n_rows, n_cols),
        out_shape=(
            jax.ShapeDtypeStruct((OWN, WIDTH), f32),
            jax.ShapeDtypeStruct((OWN, ELEMS), f32),
        ),
        in_specs=[smem, smem] + [hbm] * 8,
        out_specs=(vmem, vmem),
        scratch_shapes=[
            pltpu.VMEM((2 * OWN, WIDTH), f32),
            pltpu.VMEM((2 * OWN, WIDTH), f32),
            pltpu.VMEM((2, near_pairs.shape[0]), jnp.int32),
            pltpu.VMEM((2, far_slots), jnp.int32),
            pltpu.VMEM((OWN, ELEMS), jnp.int32),
            pltpu.VMEM((OWN, ELEMS), f32),
            pltpu.VMEM((6, OWN + 8, LANES), f32),
            pltpu.VMEM((3, OWN, LANES), f32),
            pltpu.VMEM((4, 24 * GROUPS, LANES), f32),
            pltpu.VMEM((OWN, ELEMS, 24), bf16),
            pltpu.VMEM((OWN, ELEMS, 8), f32),
            pltpu.VMEM((6, 24 * GROUPS, LANES), f32),
            pltpu.VMEM((6, 24 * GROUPS, LANES), f32),
            pltpu.VMEM((6, 8 * GROUPS, LANES), f32),
            pltpu.VMEM((6, 8 * GROUPS, LANES), f32),
            pltpu.VMEM((6, OWN, LANES), f32),
            pltpu.VMEM((3, OWN, LANES), f32),
            pltpu.VMEM((OWN, RANK, WIDTH), bf16),
            pltpu.VMEM((RANK, RANK, far_slots), bf16),
            pltpu.VMEM((n_rows * OWN // 2, 2 * RANK), bf16),
            pltpu.VMEM((RANK, far_slots), bf16),
            pltpu.VMEM((n_cols * OWN // 2, 2 * RANK), bf16),
            pltpu.VMEM((n_cols * OWN // 2, 2 * RANK), bf16),
            pltpu.SemaphoreType.DMA((8,)),
            pltpu.SemaphoreType.DMA((4,)),
            pltpu.SemaphoreType.DMA((4,)),
            pltpu.SemaphoreType.DMA((n_rows - 1,)),
            pltpu.SemaphoreType.DMA((n_rows - 1,)),
            pltpu.SemaphoreType.DMA((n_cols - 1,)),
            pltpu.SemaphoreType.DMA((n_cols - 1,)),
        ],
        compiler_params=pltpu.CompilerParams(
            collective_id=0, has_side_effects=True, vmem_limit_bytes=60 * 1024 * 1024
        ),
        name="traction",
    )(
        near_count,
        far_count,
        displacement,
        positions,
        near_pairs.T,
        far_pairs.T,
        intact,
        stiffness,
        jnp.transpose(cluster_basis, (0, 2, 1)),
        jnp.transpose(far_blocks, (1, 2, 0)),
    )


def solution(mesh):
    both = ("rows", "cols")
    in_specs = (
        P(both, None),
        P(both, None),
        P(both, None, None),
        P(both, None),
        P(both),
        P(both, None),
        P(both),
        P(both, None, None),
        P(both, None),
        P(both, None),
    )
    out_specs = (P(both, None), P(both, None))
    return jax.shard_map(local, mesh=mesh, in_specs=in_specs, out_specs=out_specs, check_vma=False)
```

```python
import functools

import jax
import jax.numpy as jnp
from jax import lax
from jax.experimental import pallas as pl
from jax.experimental.pallas import tpu as pltpu
from jax.sharding import PartitionSpec as P

LOGICAL = pl.DeviceIdType.LOGICAL
ELEMS = 96
RANK = 64
OWN = 64
WIDTH = 3 * ELEMS
LANES = 128
GROUPS = OWN // 4
core_square = 0.25
softening = 1.5

PIECES = ((0, 0), (0, 1), (1, 0), (1, 1), (0, 2), (2, 0))
SEEN = (range(0, 4), range(0, 5), range(1, 6), range(2, 6))


def mega(
    n_rows,
    n_cols,
    near_count,
    far_count,
    disp_hbm,
    pos_hbm,
    near_pairs_hbm,
    far_pairs_hbm,
    intact_hbm,
    stiffness_hbm,
    basis_hbm,
    far_hbm,
    net_out,
    damage_out,
    ext_disp,
    ext_pos,
    near_pairs,
    far_pairs,
    intact,
    stiffness,
    wide,
    centred,
    left,
    lefts,
    sums,
    right_q,
    right_s,
    disp_rows,
    pos_rows,
    weights,
    near_rows,
    basis,
    far_blocks,
    column,
    coupled,
    partial,
    arrived,
    local_sem,
    halo_send,
    halo_recv,
    gather_send,
    gather_recv,
    scatter_send,
    scatter_recv,
):
    f32, bf16 = jnp.float32, jnp.bfloat16
    i, j = lax.axis_index("rows"), lax.axis_index("cols")
    me = i * n_cols + j
    devices = n_rows * n_cols
    next_id = lax.rem(me + 1, devices)
    last_id = lax.rem(me + devices - 1, devices)
    row_peers = [lax.rem(me + d * n_cols, devices) for d in range(1, n_rows)]
    col_places = [lax.rem(j + d, n_cols) for d in range(1, n_cols)]
    col_peers = [i * n_cols + place for place in col_places]

    own = pl.ds(0, OWN)
    loads = [
        pltpu.make_async_copy(src, dst, local_sem.at[n])
        for n, (src, dst) in enumerate(
            (
                (disp_hbm, ext_disp.at[own, :]),
                (pos_hbm, ext_pos.at[own, :]),
                (near_pairs_hbm, near_pairs),
                (basis_hbm, basis),
                (far_pairs_hbm, far_pairs),
                (intact_hbm, intact),
                (stiffness_hbm, stiffness),
                (far_hbm, far_blocks),
            )
        )
    ]
    for copy in loads:
        copy.start()
    barrier = pltpu.get_barrier_semaphore()
    peers = row_peers + col_peers + [next_id, last_id]
    for peer in peers:
        pl.semaphore_signal(barrier, inc=1, device_id=peer, device_id_type=LOGICAL)

    for copy in loads[:3]:
        copy.wait()

    def lanes_of(c):
        return slice(c * ELEMS, (c + 1) * ELEMS)

    def thirds(x):
        high = x.astype(bf16).astype(f32)
        middle = (x - high).astype(bf16).astype(f32)
        return high, middle, (x - high) - middle

    def square_sum(x):
        return x[0] * x[0] + x[1] * x[1] + x[2] * x[2]

    gap = jnp.zeros((GROUPS, LANES - ELEMS), f32)
    one = jnp.ones((GROUPS, LANES), f32)
    none = jnp.zeros((GROUPS, LANES), f32)

    def rows_of(n, stride):
        return pl.ds(n, GROUPS, stride=stride)

    def block_of(n):
        return slice(GROUPS * n, GROUPS * (n + 1))

    def widen(n, ext, c, halo):
        wide[n, 2 : OWN + 2, 0:ELEMS] = ext[0:OWN, lanes_of(c)]
        if halo:
            wide[n, 0:2, 0:ELEMS] = ext[126:128, lanes_of(c)]
            wide[n, OWN + 2 : OWN + 4, 0:ELEMS] = ext[OWN : OWN + 2, lanes_of(c)]

    def build(halo):
        for c in range(3):
            widen(c, ext_pos, c, halo)
            widen(3 + c, ext_disp, c, halo)
        centre = []
        for c in range(3):
            inner = wide[c, rows_of(3, 4), :][:, :ELEMS] + wide[c, rows_of(4, 4), :][:, :ELEMS]
            centre.append(jnp.sum(inner, axis=1, keepdims=True) * (0.5 / ELEMS))
        if not halo:
            for m in range(4):
                x = [wide[c, rows_of(2 + m, 4), :][:, :ELEMS] - centre[c] for c in range(3)]
                x = [jnp.concatenate([v, gap], axis=1) for v in x]
                parts = [thirds(v) for v in x]
                norm = thirds(square_sum(x))
                for c in range(3):
                    centred[c, rows_of(m, 4), :] = x[c]
                    for n, (a, _) in enumerate(PIECES):
                        left[m, block_of(3 * n + c), :] = parts[c][a]
                for n in range(3):
                    left[m, block_of(18 + n), :] = one
                    left[m, block_of(21 + n), :] = norm[n]

        def packed(n, half):
            a0, a1, a2, a3 = [wide[n, rows_of(4 * half + m, 4), :][:, :ELEMS] for m in range(4)]
            return (
                jnp.concatenate([a0, a1[:, :32]], axis=1),
                jnp.concatenate([a1[:, 32:], a2[:, :64]], axis=1),
                jnp.concatenate([a2[:, 64:], a3], axis=1),
            )

        for half in range(2):
            sources = [packed(n, half) for n in range(6)]
            for v in range(3):
                if halo and v == 2 - 2 * half:
                    continue
                w = 3 * half + v
                y = [sources[c][v] - centre[c] for c in range(3)]
                u = [sources[3 + c][v] for c in range(3)]
                y_parts = [thirds(value) for value in y]
                u_parts = [thirds(value) for value in u]
                norm = thirds(square_sum(y) + core_square)
                inner = thirds(y[0] * u[0] + y[1] * u[1] + y[2] * u[2])
                for c in range(3):
                    for n, (_, b) in enumerate(PIECES):
                        right_q[w, block_of(3 * n + c), :] = -2.0 * y_parts[c][b]
                        right_s[w, block_of(3 * n + c), :] = u_parts[c][b]
                    triple = thirds(3.0 * y[c])
                    for n in range(2):
                        disp_rows[w, block_of(4 * n + c), :] = u_parts[c][n]
                        pos_rows[w, block_of(4 * n + c), :] = triple[n]
                for n in range(3):
                    right_q[w, block_of(18 + n), :] = norm[n]
                    right_s[w, block_of(18 + n), :] = -inner[n]
                    right_q[w, block_of(21 + n), :] = one
                    right_s[w, block_of(21 + n), :] = none
                for n in (3, 7):
                    disp_rows[w, block_of(n), :] = none
                    pos_rows[w, block_of(n), :] = 3.0 * one if n == 3 else none

    wide[...] = jnp.zeros_like(wide)
    build(False)

    slots = near_pairs.shape[1]
    near_target = near_pairs[0:1, :]
    live = lax.broadcasted_iota(jnp.int32, (1, slots), 1) < near_count[0]
    place = near_pairs[1:2, :] - near_target // 4 * 4
    row_is = lax.broadcasted_iota(jnp.int32, (OWN, slots), 0) == jnp.where(live, near_target, -1)
    lane_is = lax.broadcasted_iota(jnp.int32, (8 * ELEMS, slots), 0) // ELEMS == place
    row_is = row_is.astype(f32).astype(bf16)
    for w in range(6):
        weights[w] = lax.dot_general(
            row_is,
            lane_is[w * LANES : (w + 1) * LANES].astype(f32).astype(bf16),
            (((1,), (1,)), ((), ())),
            preferred_element_type=f32,
        )

    def halves(x):
        high = x.astype(bf16)
        return high, (x - high.astype(f32)).astype(bf16)

    def turn(g):
        for m in range(4):
            lefts[4 * g + m] = left[m, pl.ds(g, 24, stride=GROUPS), :].T[:ELEMS].astype(bf16)

    def settle(g):
        for m in range(4):
            row = pl.ds(4 * g + m, 1)
            total = sums[4 * g + m].T
            total = total[0:4] + total[4:8]
            for c in range(3):
                near_rows[c, row, 0:ELEMS] = total[c : c + 1] - centred[c, row, 0:ELEMS] * total[3:4]

    turn(0)
    turn(1)

    def near_groups(first, last):
        def near_group(g, _):
            group = pl.ds(g, 24, stride=GROUPS)
            eight = pl.ds(g, 8, stride=GROUPS)
            rows, boths = [], []
            for w in range(6):
                right = jnp.concatenate([right_q[w, group, :], right_s[w, group, :]], axis=1).astype(bf16)
                u_rows = disp_rows[w, eight, :].astype(bf16)
                y_rows = pos_rows[w, eight, :].astype(bf16)
                rows.append(jnp.concatenate([u_rows, u_rows, y_rows, y_rows], axis=1))
                seen = [m for m in range(4) if w in SEEN[m]]
                mine = jnp.concatenate([lefts[4 * g + m] for m in seen], axis=0)
                both = jnp.dot(mine, right, preferred_element_type=f32)
                boths.append({m: both[at * ELEMS : (at + 1) * ELEMS] for at, m in enumerate(seen)})
            totals = [None] * 4
            for n in range(5):
                for pair in range(2):
                    w = n + pair
                    seen = [m for m in (2 * pair, 2 * pair + 1) if w in SEEN[m]]
                    values = []
                    for m in seen:
                        part = boths[w][m]
                        inverse = lax.rsqrt(jnp.maximum(part[:, :LANES], core_square))
                        square = inverse * inverse
                        cube = square * (inverse * weights[w, pl.ds(4 * g + m, 1), :])
                        pull = (part[:, LANES:] * square) * cube
                        values.append(jnp.concatenate(halves(cube) + halves(pull), axis=1))
                    added = lax.dot_general(
                        jnp.concatenate(values, axis=0), rows[w], (((1,), (1,)), ((), ())), preferred_element_type=f32
                    )
                    for at, m in enumerate(seen):
                        piece = added[at * ELEMS : (at + 1) * ELEMS]
                        totals[m] = piece if totals[m] is None else totals[m] + piece
            settle(jnp.maximum(g - 1, 0))
            for m in range(4):
                sums[4 * g + m] = totals[m]
            turn(jnp.minimum(g + 1, GROUPS - 1))
            return 0

        lax.fori_loop(first, last, near_group, 0)
        settle(last - 1)

    loads[3].wait()

    def project(block, coeff):
        top = pl.multiple_of(block * 8, 8)
        rows = ext_disp[pl.ds(top, 8), :].astype(bf16)
        lane = lax.broadcasted_iota(jnp.int32, (RANK, OWN), 1)
        for n in range(8):
            product = basis[top + n] * rows[n : n + 1, :]
            product = product[:, :LANES].astype(f32) + product[:, LANES : 2 * LANES].astype(f32) + jnp.concatenate(
                [product[:, 2 * LANES :].astype(f32), jnp.zeros((RANK, 3 * LANES - WIDTH), f32)], axis=1
            )
            coeff = jnp.where(lane == top + n, jnp.sum(product, axis=1, keepdims=True), coeff)
        return coeff

    coeff = lax.fori_loop(0, OWN // 8, project, jnp.zeros((RANK, OWN), f32))
    half = OWN // 2

    def pack(block):
        return jnp.concatenate([block[:half], block[half:]], axis=1).astype(bf16)

    own_rows = pl.ds(pl.multiple_of(i * half, half), half)
    column[own_rows, :] = pack(coeff)

    z = lax.rem(j, 4) * 2 + i // (n_rows // 2)
    sent = 8 - jnp.minimum(z, 4) * 3 // 2
    gathered_at = sent + jnp.where(z == 0, 4, 5)
    near_groups(1, sent)
    pl.semaphore_wait(barrier, len(peers))

    def remote(src, dst, send, recv, peer):
        return pltpu.make_async_remote_copy(
            src_ref=src, dst_ref=dst, send_sem=send, recv_sem=recv, device_id=peer, device_id_type=LOGICAL
        )

    mine = column.at[own_rows, :]
    gathers = [
        remote(mine, mine, gather_send.at[d], gather_recv.at[d], peer) for d, peer in enumerate(row_peers)
    ]
    halos = []
    for n, (src, dst) in enumerate(((disp_hbm, ext_disp), (pos_hbm, ext_pos))):
        halos.append(remote(src.at[pl.ds(OWN - 8, 8), :], dst.at[pl.ds(120, 8), :], halo_send.at[n], halo_recv.at[n], next_id))
        halos.append(remote(src.at[pl.ds(0, 8), :], dst.at[pl.ds(OWN, 8), :], halo_send.at[2 + n], halo_recv.at[2 + n], last_id))
    for copy in gathers + halos:
        copy.start()

    near_groups(sent, gathered_at)

    for copy in gathers:
        copy.wait()
    for copy in loads[4:]:
        copy.wait()
    tops = [column[n * half : (n + 1) * half, :RANK] for n in range(n_rows)]
    bottoms = [column[n * half : (n + 1) * half, RANK:] for n in range(n_rows)]
    column_turned = jnp.concatenate(
        [jnp.concatenate(tops, axis=1), jnp.concatenate(bottoms, axis=1)], axis=0
    )
    far_slots = far_pairs.shape[1]
    sources = n_rows * OWN

    wide_block = 2 * LANES
    sublane = lax.broadcasted_iota(jnp.int32, (8, wide_block), 0)

    def merge(blocks):
        reach = 4
        while len(blocks) > 1:
            upper = sublane // reach % 2 == 0
            count = len(blocks) // 2
            pairs = [(blocks[n], blocks[n + count]) for n in range(count)]
            blocks = []
            for x, y in pairs:
                crossed = jnp.where(upper, y, x)
                moved = pltpu.roll(crossed, reach, axis=0)
                if reach < 4:
                    moved = jnp.where(upper, pltpu.roll(crossed, 8 - reach, axis=0), moved)
                blocks.append(jnp.where(upper, x, y) + moved)
            reach //= 2
        return blocks[0]

    def couple(block, _):
        first = pl.multiple_of(block * wide_block, wide_block)
        source = far_pairs[1:2, pl.ds(first, wide_block)]
        alive = lax.broadcasted_iota(jnp.int32, (1, wide_block), 1) + first < far_count[0]
        source = jnp.where(alive, source, -1)
        chosen = (lax.broadcasted_iota(jnp.int32, (sources, wide_block), 0) == source).astype(f32).astype(bf16)
        gathered = jnp.dot(column_turned, chosen, preferred_element_type=f32).astype(bf16)

        def ranks(part, _):
            top = pl.multiple_of(part * 16, 16)
            summed = []
            for n in range(16):
                product = far_blocks[top + n, :, pl.ds(first, wide_block)] * gathered
                product = ((product[0:16] + product[16:32]) + (product[32:48] + product[48:64])).astype(f32)
                summed.append(product[0:8] + product[8:16])
            whole = jnp.concatenate([merge(summed[:8]), merge(summed[8:])], axis=0)
            coupled[pl.ds(top, 16), pl.ds(first, wide_block)] = whole.astype(bf16)
            return 0

        return lax.fori_loop(0, RANK // 16, ranks, 0)

    lax.fori_loop(0, far_slots // wide_block, couple, 0)

    def collect(block, _):
        first = pl.multiple_of(block * wide_block, wide_block)
        chosen = lax.broadcasted_iota(jnp.int32, (wide_block, far_slots), 0) + first == far_pairs[0:1, :]
        found = lax.dot_general(
            chosen.astype(f32).astype(bf16), coupled[...], (((1,), (1,)), ((), ())), preferred_element_type=f32
        )
        for n in range(wide_block // OWN):
            to = pl.multiple_of(block * (wide_block // 2) + n * half, half)
            partial[pl.ds(to, half), :] = pack(found[n * OWN : (n + 1) * OWN])
        return 0

    lax.fori_loop(0, n_cols * OWN // wide_block, collect, 0)

    for copy in halos:
        copy.wait()

    here = pl.ds(pl.multiple_of(j * half, half), half)
    scatters = []
    for d, peer in enumerate(col_peers):
        block = partial.at[pl.ds(pl.multiple_of(col_places[d] * half, half), half), :]
        scatters.append(remote(block, arrived.at[here, :], scatter_send.at[d], scatter_recv.at[d], peer))
    for copy in scatters:
        copy.start()
    arrived[here, :] = partial[here, :]

    ext_disp[OWN : OWN + 8, :] = jnp.where(me == devices - 1, 0.0, ext_disp[OWN : OWN + 8, :])
    ext_disp[120:128, :] = jnp.where(me == 0, 0.0, ext_disp[120:128, :])
    build(True)
    near_groups(gathered_at, GROUPS)
    near_groups(0, 1)

    parts = [near_rows[c, :, 0:ELEMS] for c in range(3)]
    u = [ext_disp[0:OWN, lanes_of(c)] for c in range(3)]
    separation = jnp.sqrt(1.0 + (u[0] * u[0] + u[1] * u[1] + u[2] * u[2]))
    softened = 1.0 - jnp.exp(-(separation - 1.0) / softening)
    whole_element = intact[...].astype(f32)
    damage = whole_element * softened + (1.0 - whole_element)
    damage_out[...] = damage
    held = (1.0 - damage) * stiffness[...]
    base = jnp.concatenate([parts[c] - held * u[c] for c in range(3)], axis=1)

    for copy in scatters:
        copy.wait()
    owned = arrived[0:half, :].astype(f32)
    for n in range(1, n_cols):
        owned = owned + arrived[n * half : (n + 1) * half, :].astype(f32)
    owned = owned.T
    owned = jnp.concatenate([owned[:RANK], owned[RANK:]], axis=1)
    fold = lax.broadcasted_iota(jnp.int32, (16, 256), 0) == lax.broadcasted_iota(jnp.int32, (16, 256), 1) // 16
    fold = fold.astype(f32).astype(bf16)
    for block in range(OWN // 16):
        summed = []
        for n in range(16):
            k = 16 * block + n
            product = basis[k] * owned[:, k : k + 1].astype(bf16)
            summed.append((product[0:16] + product[16:32]) + (product[32:48] + product[48:64]))
        far = jnp.dot(fold, jnp.concatenate(summed, axis=0), preferred_element_type=f32)
        net_out[16 * block : 16 * block + 16, :] = base[16 * block : 16 * block + 16] + far


def local(
    displacement,
    positions,
    cluster_basis,
    near_pairs,
    near_count,
    far_pairs,
    far_count,
    far_blocks,
    intact,
    stiffness,
):
    n_rows, n_cols = lax.axis_size("rows"), lax.axis_size("cols")
    f32, bf16 = jnp.float32, jnp.bfloat16
    far_slots = far_pairs.shape[0]
    vmem = pl.BlockSpec(memory_space=pltpu.VMEM)
    smem = pl.BlockSpec(memory_space=pltpu.SMEM)
    hbm = pl.BlockSpec(memory_space=pltpu.HBM)
    return pl.pallas_call(
        functools.partial(mega, n_rows, n_cols),
        out_shape=(
            jax.ShapeDtypeStruct((OWN, WIDTH), f32),
            jax.ShapeDtypeStruct((OWN, ELEMS), f32),
        ),
        in_specs=[smem] * 2 + [hbm] * 8,
        out_specs=(vmem, vmem),
        scratch_shapes=[
            pltpu.VMEM((2 * OWN, WIDTH), f32),
            pltpu.VMEM((2 * OWN, WIDTH), f32),
            pltpu.VMEM((2, near_pairs.shape[0]), jnp.int32),
            pltpu.VMEM((2, far_slots), jnp.int32),
            pltpu.VMEM((OWN, ELEMS), jnp.int32),
            pltpu.VMEM((OWN, ELEMS), f32),
            pltpu.VMEM((6, OWN + 8, LANES), f32),
            pltpu.VMEM((3, OWN, LANES), f32),
            pltpu.VMEM((4, 24 * GROUPS, LANES), f32),
            pltpu.VMEM((OWN, ELEMS, 24), bf16),
            pltpu.VMEM((OWN, ELEMS, 8), f32),
            pltpu.VMEM((6, 24 * GROUPS, LANES), f32),
            pltpu.VMEM((6, 24 * GROUPS, LANES), f32),
            pltpu.VMEM((6, 8 * GROUPS, LANES), f32),
            pltpu.VMEM((6, 8 * GROUPS, LANES), f32),
            pltpu.VMEM((6, OWN, LANES), f32),
            pltpu.VMEM((3, OWN, LANES), f32),
            pltpu.VMEM((OWN, RANK, WIDTH), bf16),
            pltpu.VMEM((RANK, RANK, far_slots), bf16),
            pltpu.VMEM((n_rows * OWN // 2, 2 * RANK), bf16),
            pltpu.VMEM((RANK, far_slots), bf16),
            pltpu.VMEM((n_cols * OWN // 2, 2 * RANK), bf16),
            pltpu.VMEM((n_cols * OWN // 2, 2 * RANK), bf16),
            pltpu.SemaphoreType.DMA((8,)),
            pltpu.SemaphoreType.DMA((4,)),
            pltpu.SemaphoreType.DMA((4,)),
            pltpu.SemaphoreType.DMA((n_rows - 1,)),
            pltpu.SemaphoreType.DMA((n_rows - 1,)),
            pltpu.SemaphoreType.DMA((n_cols - 1,)),
            pltpu.SemaphoreType.DMA((n_cols - 1,)),
        ],
        compiler_params=pltpu.CompilerParams(
            collective_id=0, has_side_effects=True, vmem_limit_bytes=34 * 1024 * 1024
        ),
        name="traction",
    )(
        near_count,
        far_count,
        *[
            pltpu.with_memory_space_constraint(x, pltpu.HBM)
            for x in (
                displacement,
                positions,
                near_pairs.T,
                far_pairs.T,
                intact,
                stiffness,
                jnp.transpose(cluster_basis, (0, 2, 1)),
                jnp.transpose(far_blocks, (1, 2, 0)),
            )
        ],
    )


def solution(mesh):
    both = ("rows", "cols")
    in_specs = (
        P(both, None),
        P(both, None),
        P(both, None, None),
        P(both, None),
        P(both),
        P(both, None),
        P(both),
        P(both, None, None),
        P(both, None),
        P(both, None),
    )
    out_specs = (P(both, None), P(both, None))
    return jax.shard_map(local, mesh=mesh, in_specs=in_specs, out_specs=out_specs, check_vma=False)
```

```python
import functools

import jax
import jax.numpy as jnp
from jax import lax
from jax.experimental import pallas as pl
from jax.experimental.pallas import tpu as pltpu
from jax.sharding import PartitionSpec as P

LOGICAL = pl.DeviceIdType.LOGICAL
ELEMS = 96
RANK = 64
OWN = 64
WIDTH = 3 * ELEMS
LANES = 128
GROUPS = OWN // 4
core_square = 0.25
softening = 1.5

PIECES = ((0, 0), (0, 1), (1, 0), (1, 1), (0, 2), (2, 0))
PLAIN = (1,)
SEEN = (range(0, 4), range(0, 5), range(1, 6), range(2, 6))


def mega(
    n_rows,
    n_cols,
    near_count,
    far_count,
    disp_hbm,
    pos_hbm,
    near_pairs_hbm,
    far_pairs_hbm,
    intact_hbm,
    stiffness_hbm,
    basis_hbm,
    far_hbm,
    net_out,
    damage_out,
    ext_disp,
    ext_pos,
    near_pairs,
    far_pairs,
    intact,
    stiffness,
    wide,
    centred,
    left,
    lefts,
    held,
    sums,
    right_q,
    right_s,
    disp_rows,
    pos_rows,
    disp_f,
    pos_f,
    weights,
    near_rows,
    basis,
    far_blocks,
    column,
    coupled,
    partial,
    arrived,
    local_sem,
    halo_send,
    halo_recv,
    gather_send,
    gather_recv,
    scatter_send,
    scatter_recv,
):
    f32, bf16 = jnp.float32, jnp.bfloat16
    i, j = lax.axis_index("rows"), lax.axis_index("cols")
    me = i * n_cols + j
    devices = n_rows * n_cols
    next_id = lax.rem(me + 1, devices)
    last_id = lax.rem(me + devices - 1, devices)
    row_peers = [lax.rem(me + d * n_cols, devices) for d in range(1, n_rows)]
    col_places = [lax.rem(j + d, n_cols) for d in range(1, n_cols)]
    col_peers = [i * n_cols + place for place in col_places]

    own = pl.ds(0, OWN)
    loads = [
        pltpu.make_async_copy(src, dst, local_sem.at[n])
        for n, (src, dst) in enumerate(
            (
                (disp_hbm, ext_disp.at[own, :]),
                (pos_hbm, ext_pos.at[own, :]),
                (near_pairs_hbm, near_pairs),
                (basis_hbm, basis),
                (far_pairs_hbm, far_pairs),
                (intact_hbm, intact),
                (stiffness_hbm, stiffness),
                (far_hbm, far_blocks),
            )
        )
    ]
    for copy in loads:
        copy.start()
    barrier = pltpu.get_barrier_semaphore()
    peers = row_peers + col_peers + [next_id, last_id]
    for peer in peers:
        pl.semaphore_signal(barrier, inc=1, device_id=peer, device_id_type=LOGICAL)

    for n in range(6):
        wide[n, 0:8, :] = jnp.zeros((8, LANES), jnp.float32)
        wide[n, OWN : OWN + 8, :] = jnp.zeros((8, LANES), jnp.float32)
    for copy in loads[:3]:
        copy.wait()

    def lanes_of(c):
        return slice(c * ELEMS, (c + 1) * ELEMS)

    def thirds(x):
        high = x.astype(bf16).astype(f32)
        middle = (x - high).astype(bf16).astype(f32)
        return high, middle, (x - high) - middle

    def square_sum(x):
        return x[0] * x[0] + x[1] * x[1] + x[2] * x[2]

    gap = jnp.zeros((GROUPS, LANES - ELEMS), f32)
    one = jnp.ones((GROUPS, LANES), f32)
    none = jnp.zeros((GROUPS, LANES), f32)

    def rows_of(n, stride):
        return pl.ds(n, GROUPS, stride=stride)

    def block_of(n):
        return slice(GROUPS * n, GROUPS * (n + 1))

    def widen(n, ext, c, halo):
        wide[n, 2 : OWN + 2, 0:ELEMS] = ext[0:OWN, lanes_of(c)]
        if halo:
            wide[n, 0:2, 0:ELEMS] = ext[126:128, lanes_of(c)]
            wide[n, OWN + 2 : OWN + 4, 0:ELEMS] = ext[OWN : OWN + 2, lanes_of(c)]

    def build(halo):
        for c in range(3):
            widen(c, ext_pos, c, halo)
            widen(3 + c, ext_disp, c, halo)
        centre = []
        for c in range(3):
            inner = wide[c, rows_of(3, 4), :][:, :ELEMS] + wide[c, rows_of(4, 4), :][:, :ELEMS]
            centre.append(jnp.sum(inner, axis=1, keepdims=True) * (0.5 / ELEMS))
        if not halo:
            for m in range(4):
                x = [wide[c, rows_of(2 + m, 4), :][:, :ELEMS] - centre[c] for c in range(3)]
                x = [jnp.concatenate([v, gap], axis=1) for v in x]
                parts = [thirds(v) for v in x]
                norm = thirds(square_sum(x))
                for c in range(3):
                    centred[c, rows_of(m, 4), :] = x[c]
                    for n, (a, _) in enumerate(PIECES):
                        left[m, block_of(3 * n + c), :] = parts[c][a]
                for n in range(3):
                    left[m, block_of(18 + n), :] = one
                    left[m, block_of(21 + n), :] = norm[n]

        def packed(n, half):
            a0, a1, a2, a3 = [wide[n, rows_of(4 * half + m, 4), :][:, :ELEMS] for m in range(4)]
            return (
                jnp.concatenate([a0, a1[:, :32]], axis=1),
                jnp.concatenate([a1[:, 32:], a2[:, :64]], axis=1),
                jnp.concatenate([a2[:, 64:], a3], axis=1),
            )

        for half in range(2):
            sources = [packed(n, half) for n in range(6)]
            for v in range(3):
                if halo and v == 2 - 2 * half:
                    continue
                w = 3 * half + v
                y = [sources[c][v] - centre[c] for c in range(3)]
                u = [sources[3 + c][v] for c in range(3)]
                y_parts = [thirds(value) for value in y]
                u_parts = [thirds(value) for value in u]
                norm = thirds(square_sum(y) + core_square)
                inner = thirds(y[0] * u[0] + y[1] * u[1] + y[2] * u[2])
                for c in range(3):
                    for n, (_, b) in enumerate(PIECES):
                        right_q[w, block_of(3 * n + c), :] = -2.0 * y_parts[c][b]
                        right_s[w, block_of(3 * n + c), :] = u_parts[c][b]
                    disp_f[w, block_of(c), :] = u[c]
                    pos_f[w, block_of(c), :] = 3.0 * y[c]
                    triple = thirds(3.0 * y[c])
                    for n in range(2):
                        disp_rows[w, block_of(4 * n + c), :] = u_parts[c][n]
                        pos_rows[w, block_of(4 * n + c), :] = triple[n]
                for n in range(3):
                    right_q[w, block_of(18 + n), :] = norm[n]
                    right_s[w, block_of(18 + n), :] = -inner[n]
                    right_q[w, block_of(21 + n), :] = one
                    right_s[w, block_of(21 + n), :] = none
                for n in (3, 7):
                    disp_rows[w, block_of(n), :] = none
                    pos_rows[w, block_of(n), :] = 3.0 * one if n == 3 else none

    build(False)

    slots = near_pairs.shape[1]
    near_target = near_pairs[0:1, :]
    live = lax.broadcasted_iota(jnp.int32, (1, slots), 1) < near_count[0]
    place = near_pairs[1:2, :] - near_target // 4 * 4
    row_is = lax.broadcasted_iota(jnp.int32, (OWN, slots), 0) == jnp.where(live, near_target, -1)
    lane_is = lax.broadcasted_iota(jnp.int32, (8 * ELEMS, slots), 0) // ELEMS == place
    row_is = row_is.astype(f32).astype(bf16)
    for w in range(6):
        weights[w] = lax.dot_general(
            row_is,
            lane_is[w * LANES : (w + 1) * LANES].astype(f32).astype(bf16),
            (((1,), (1,)), ((), ())),
            preferred_element_type=f32,
        )

    def halves(x):
        high = x.astype(bf16)
        return high, (x - high.astype(f32)).astype(bf16)

    def turn(g):
        for m in range(4):
            lefts[4 * g + m] = left[m, pl.ds(g, 24, stride=GROUPS), :].T[:ELEMS].astype(bf16)

    def settle(g):
        for m in range(4):
            row = pl.ds(4 * g + m, 1)
            total = sums[4 * g + m].T
            total = total[0:4] + total[4:8]
            for c in range(3):
                near_rows[c, row, 0:ELEMS] = total[c : c + 1] - centred[c, row, 0:ELEMS] * total[3:4]

    def meet(g, w):
        group = pl.ds(g, 24, stride=GROUPS)
        right = jnp.concatenate([right_q[w, group, :], right_s[w, group, :]], axis=1).astype(bf16)
        seen = [m for m in range(4) if w in SEEN[m]]
        mine = jnp.concatenate([lefts[4 * g + m] for m in seen], axis=0)
        both = jnp.dot(mine, right, preferred_element_type=f32)
        for at, m in enumerate(seen):
            held[6 * m + w] = both[at * ELEMS : (at + 1) * ELEMS]

    def near_groups(first, last):
        def near_group(t, _):
            g = lax.rem(t + 1, GROUPS)
            eight = pl.ds(g, 8, stride=GROUPS)
            rows = []
            for w in range(6):
                u_rows = disp_rows[w, eight, :].astype(bf16)
                y_rows = pos_rows[w, eight, :].astype(bf16)
                rows.append(jnp.concatenate([u_rows, u_rows, y_rows, y_rows], axis=1))
            totals = [None] * 4
            plain = {m: [jnp.zeros((ELEMS, LANES), f32)] * 4 for m in PLAIN}
            for n in range(5):
                for pair in range(2):
                    w = n + pair
                    seen = [m for m in (2 * pair, 2 * pair + 1) if w in SEEN[m]]
                    values = []
                    for m in seen:
                        part = held[6 * m + w]
                        inverse = lax.rsqrt(jnp.maximum(part[:, :LANES], core_square))
                        square = inverse * inverse
                        cube = square * (inverse * weights[w, pl.ds(4 * g + m, 1), :])
                        pull = (part[:, LANES:] * square) * cube
                        if m in PLAIN:
                            u = [disp_f[w, pl.ds(GROUPS * c + g, 1), :] for c in range(3)]
                            y = [pos_f[w, pl.ds(GROUPS * c + g, 1), :] for c in range(3)]
                            plain[m] = [plain[m][c] + (cube * u[c] + pull * y[c]) for c in range(3)] + [plain[m][3] + pull]
                        else:
                            values.append(jnp.concatenate(halves(cube) + halves(pull), axis=1))
                    seen = [m for m in seen if m not in PLAIN]
                    if not seen:
                        continue
                    added = lax.dot_general(
                        jnp.concatenate(values, axis=0), rows[w], (((1,), (1,)), ((), ())), preferred_element_type=f32
                    )
                    for at, m in enumerate(seen):
                        piece = added[at * ELEMS : (at + 1) * ELEMS]
                        totals[m] = piece if totals[m] is None else totals[m] + piece
                meet(lax.rem(t + 2, GROUPS), n)
            meet(lax.rem(t + 2, GROUPS), 5)
            lane = lax.broadcasted_iota(jnp.int32, (ELEMS, 8), 1)
            for m in PLAIN:
                columns = [jnp.sum(x, axis=1, keepdims=True) for x in plain[m]]
                columns[3] = 3.0 * columns[3]
                total = jnp.zeros((ELEMS, 8), f32)
                for c in range(4):
                    total = jnp.where(lane == c, columns[c], total)
                totals[m] = total
            settle(t)
            for m in range(4):
                sums[4 * g + m] = totals[m]
            turn(lax.rem(t + 3, GROUPS))
            return 0

        lax.fori_loop(first, last, near_group, 0)
        settle(lax.rem(last, GROUPS))

    turn(1)
    turn(2)
    for w in range(6):
        meet(1, w)

    loads[3].wait()

    def project(block, coeff):
        top = pl.multiple_of(block * 8, 8)
        rows = ext_disp[pl.ds(top, 8), :].astype(bf16)
        lane = lax.broadcasted_iota(jnp.int32, (RANK, OWN), 1)
        for n in range(8):
            product = basis[top + n] * rows[n : n + 1, :]
            product = product[:, :LANES].astype(f32) + product[:, LANES : 2 * LANES].astype(f32) + jnp.concatenate(
                [product[:, 2 * LANES :].astype(f32), jnp.zeros((RANK, 3 * LANES - WIDTH), f32)], axis=1
            )
            coeff = jnp.where(lane == top + n, jnp.sum(product, axis=1, keepdims=True), coeff)
        return coeff

    coeff = lax.fori_loop(0, OWN // 8, project, jnp.zeros((RANK, OWN), f32))
    half = OWN // 2

    def pack(block):
        return jnp.concatenate([block[:half], block[half:]], axis=1).astype(bf16)

    own_rows = pl.ds(pl.multiple_of(i * half, half), half)
    column[own_rows, :] = pack(coeff)

    z = lax.rem(j, 4) * 2 + i // (n_rows // 2)
    sent = jnp.where(z == 0, 7, jnp.where(z == 1, 6, jnp.where(z == 2, 4, jnp.where(z == 3, 3, 0))))
    gathered_at = sent + jnp.where(z < 2, 6, 5)
    near_groups(0, sent)
    pl.semaphore_wait(barrier, len(peers))

    def remote(src, dst, send, recv, peer):
        return pltpu.make_async_remote_copy(
            src_ref=src, dst_ref=dst, send_sem=send, recv_sem=recv, device_id=peer, device_id_type=LOGICAL
        )

    mine = column.at[own_rows, :]
    gathers = [
        remote(mine, mine, gather_send.at[d], gather_recv.at[d], peer) for d, peer in enumerate(row_peers)
    ]
    halos = []
    for n, (src, dst) in enumerate(((disp_hbm, ext_disp), (pos_hbm, ext_pos))):
        halos.append(remote(src.at[pl.ds(OWN - 8, 8), :], dst.at[pl.ds(120, 8), :], halo_send.at[n], halo_recv.at[n], next_id))
        halos.append(remote(src.at[pl.ds(0, 8), :], dst.at[pl.ds(OWN, 8), :], halo_send.at[2 + n], halo_recv.at[2 + n], last_id))
    for copy in gathers + halos:
        copy.start()

    near_groups(sent, gathered_at)

    for copy in gathers:
        copy.wait()
    for copy in loads[4:]:
        copy.wait()
    tops = [column[n * half : (n + 1) * half, :RANK] for n in range(n_rows)]
    bottoms = [column[n * half : (n + 1) * half, RANK:] for n in range(n_rows)]
    column_turned = jnp.concatenate(
        [jnp.concatenate(tops, axis=1), jnp.concatenate(bottoms, axis=1)], axis=0
    )
    far_slots = far_pairs.shape[1]
    sources = n_rows * OWN

    wide_block = 2 * LANES
    sublane = lax.broadcasted_iota(jnp.int32, (8, wide_block), 0)

    def merge(blocks):
        reach = 4
        while len(blocks) > 1:
            upper = sublane // reach % 2 == 0
            count = len(blocks) // 2
            pairs = [(blocks[n], blocks[n + count]) for n in range(count)]
            blocks = []
            for x, y in pairs:
                crossed = jnp.where(upper, y, x)
                moved = pltpu.roll(crossed, reach, axis=0)
                if reach < 4:
                    moved = jnp.where(upper, pltpu.roll(crossed, 8 - reach, axis=0), moved)
                blocks.append(jnp.where(upper, x, y) + moved)
            reach //= 2
        return blocks[0]

    def couple(block, _):
        first = pl.multiple_of(block * wide_block, wide_block)
        source = far_pairs[1:2, pl.ds(first, wide_block)]
        alive = lax.broadcasted_iota(jnp.int32, (1, wide_block), 1) + first < far_count[0]
        source = jnp.where(alive, source, -1)
        chosen = (lax.broadcasted_iota(jnp.int32, (sources, wide_block), 0) == source).astype(f32).astype(bf16)
        gathered = jnp.dot(column_turned, chosen, preferred_element_type=f32).astype(bf16)

        def ranks(part, _):
            top = pl.multiple_of(part * 16, 16)
            summed = []
            for n in range(16):
                product = far_blocks[top + n, :, pl.ds(first, wide_block)] * gathered
                product = ((product[0:16] + product[16:32]) + (product[32:48] + product[48:64])).astype(f32)
                summed.append(product[0:8] + product[8:16])
            whole = jnp.concatenate([merge(summed[:8]), merge(summed[8:])], axis=0)
            coupled[pl.ds(top, 16), pl.ds(first, wide_block)] = whole.astype(bf16)
            return 0

        return lax.fori_loop(0, RANK // 16, ranks, 0)

    lax.fori_loop(0, far_slots // wide_block, couple, 0)

    def collect(block, _):
        first = pl.multiple_of(block * wide_block, wide_block)
        chosen = lax.broadcasted_iota(jnp.int32, (wide_block, far_slots), 0) + first == far_pairs[0:1, :]
        found = lax.dot_general(
            chosen.astype(f32).astype(bf16), coupled[...], (((1,), (1,)), ((), ())), preferred_element_type=f32
        )
        for n in range(wide_block // OWN):
            to = pl.multiple_of(block * (wide_block // 2) + n * half, half)
            partial[pl.ds(to, half), :] = pack(found[n * OWN : (n + 1) * OWN])
        return 0

    lax.fori_loop(0, n_cols * OWN // wide_block, collect, 0)

    for copy in halos:
        copy.wait()

    here = pl.ds(pl.multiple_of(j * half, half), half)
    scatters = []
    for d, peer in enumerate(col_peers):
        block = partial.at[pl.ds(pl.multiple_of(col_places[d] * half, half), half), :]
        scatters.append(remote(block, arrived.at[here, :], scatter_send.at[d], scatter_recv.at[d], peer))
    for copy in scatters:
        copy.start()
    arrived[here, :] = partial[here, :]

    ext_disp[OWN : OWN + 8, :] = jnp.where(me == devices - 1, 0.0, ext_disp[OWN : OWN + 8, :])
    ext_disp[120:128, :] = jnp.where(me == 0, 0.0, ext_disp[120:128, :])
    build(True)
    near_groups(gathered_at, GROUPS)

    parts = [near_rows[c, :, 0:ELEMS] for c in range(3)]
    u = [ext_disp[0:OWN, lanes_of(c)] for c in range(3)]
    separation = jnp.sqrt(1.0 + (u[0] * u[0] + u[1] * u[1] + u[2] * u[2]))
    softened = 1.0 - jnp.exp(-(separation - 1.0) / softening)
    whole_element = intact[...].astype(f32)
    damage = whole_element * softened + (1.0 - whole_element)
    damage_out[...] = damage
    held = (1.0 - damage) * stiffness[...]
    base = jnp.concatenate([parts[c] - held * u[c] for c in range(3)], axis=1)

    for copy in scatters:
        copy.wait()
    owned = arrived[0:half, :].astype(f32)
    for n in range(1, n_cols):
        owned = owned + arrived[n * half : (n + 1) * half, :].astype(f32)
    owned = owned.T
    owned = jnp.concatenate([owned[:RANK], owned[RANK:]], axis=1)
    fold = lax.broadcasted_iota(jnp.int32, (16, 256), 0) == lax.broadcasted_iota(jnp.int32, (16, 256), 1) // 16
    fold = fold.astype(f32).astype(bf16)
    for block in range(OWN // 16):
        summed = []
        for n in range(16):
            k = 16 * block + n
            product = basis[k] * owned[:, k : k + 1].astype(bf16)
            summed.append((product[0:16] + product[16:32]) + (product[32:48] + product[48:64]))
        far = jnp.dot(fold, jnp.concatenate(summed, axis=0), preferred_element_type=f32)
        net_out[16 * block : 16 * block + 16, :] = base[16 * block : 16 * block + 16] + far


def local(
    displacement,
    positions,
    cluster_basis,
    near_pairs,
    near_count,
    far_pairs,
    far_count,
    far_blocks,
    intact,
    stiffness,
):
    n_rows, n_cols = lax.axis_size("rows"), lax.axis_size("cols")
    f32, bf16 = jnp.float32, jnp.bfloat16
    far_slots = far_pairs.shape[0]
    vmem = pl.BlockSpec(memory_space=pltpu.VMEM)
    smem = pl.BlockSpec(memory_space=pltpu.SMEM)
    hbm = pl.BlockSpec(memory_space=pltpu.HBM)
    return pl.pallas_call(
        functools.partial(mega, n_rows, n_cols),
        out_shape=(
            jax.ShapeDtypeStruct((OWN, WIDTH), f32),
            jax.ShapeDtypeStruct((OWN, ELEMS), f32),
        ),
        in_specs=[smem] * 2 + [hbm] * 8,
        out_specs=(vmem, vmem),
        scratch_shapes=[
            pltpu.VMEM((2 * OWN, WIDTH), f32),
            pltpu.VMEM((2 * OWN, WIDTH), f32),
            pltpu.VMEM((2, near_pairs.shape[0]), jnp.int32),
            pltpu.VMEM((2, far_slots), jnp.int32),
            pltpu.VMEM((OWN, ELEMS), jnp.int32),
            pltpu.VMEM((OWN, ELEMS), f32),
            pltpu.VMEM((6, OWN + 8, LANES), f32),
            pltpu.VMEM((3, OWN, LANES), f32),
            pltpu.VMEM((4, 24 * GROUPS, LANES), f32),
            pltpu.VMEM((OWN, ELEMS, 24), bf16),
            pltpu.VMEM((24, ELEMS, 2 * LANES), f32),
            pltpu.VMEM((OWN, ELEMS, 8), f32),
            pltpu.VMEM((6, 24 * GROUPS, LANES), f32),
            pltpu.VMEM((6, 24 * GROUPS, LANES), f32),
            pltpu.VMEM((6, 8 * GROUPS, LANES), f32),
            pltpu.VMEM((6, 8 * GROUPS, LANES), f32),
            pltpu.VMEM((6, 3 * GROUPS, LANES), f32),
            pltpu.VMEM((6, 3 * GROUPS, LANES), f32),
            pltpu.VMEM((6, OWN, LANES), f32),
            pltpu.VMEM((3, OWN, LANES), f32),
            pltpu.VMEM((OWN, RANK, WIDTH), bf16),
            pltpu.VMEM((RANK, RANK, far_slots), bf16),
            pltpu.VMEM((n_rows * OWN // 2, 2 * RANK), bf16),
            pltpu.VMEM((RANK, far_slots), bf16),
            pltpu.VMEM((n_cols * OWN // 2, 2 * RANK), bf16),
            pltpu.VMEM((n_cols * OWN // 2, 2 * RANK), bf16),
            pltpu.SemaphoreType.DMA((8,)),
            pltpu.SemaphoreType.DMA((4,)),
            pltpu.SemaphoreType.DMA((4,)),
            pltpu.SemaphoreType.DMA((n_rows - 1,)),
            pltpu.SemaphoreType.DMA((n_rows - 1,)),
            pltpu.SemaphoreType.DMA((n_cols - 1,)),
            pltpu.SemaphoreType.DMA((n_cols - 1,)),
        ],
        compiler_params=pltpu.CompilerParams(
            collective_id=0, has_side_effects=True, vmem_limit_bytes=40 * 1024 * 1024
        ),
        name="traction",
    )(
        near_count,
        far_count,
        *[
            pltpu.with_memory_space_constraint(x, pltpu.HBM)
            for x in (
                displacement,
                positions,
                near_pairs.T,
                far_pairs.T,
                intact,
                stiffness,
                jnp.transpose(cluster_basis, (0, 2, 1)),
                jnp.transpose(far_blocks, (1, 2, 0)),
            )
        ],
    )


def solution(mesh):
    both = ("rows", "cols")
    in_specs = (
        P(both, None),
        P(both, None),
        P(both, None, None),
        P(both, None),
        P(both),
        P(both, None),
        P(both),
        P(both, None, None),
        P(both, None),
        P(both, None),
    )
    out_specs = (P(both, None), P(both, None))
    return jax.shard_map(local, mesh=mesh, in_specs=in_specs, out_specs=out_specs, check_vma=False)
```

```python
import functools

import jax
import jax.numpy as jnp
from jax import lax
from jax.experimental import pallas as pl
from jax.experimental.pallas import tpu as pltpu
from jax.sharding import PartitionSpec as P

LOGICAL = pl.DeviceIdType.LOGICAL
ELEMS = 96
RANK = 64
OWN = 64
WIDTH = 3 * ELEMS
LANES = 128
GROUPS = OWN // 4
core_square = 0.25
softening = 1.5

PIECES = ((0, 0), (0, 1), (1, 0), (1, 1), (0, 2), (2, 0))
PLAIN = (1,)
SEEN = (range(0, 4), range(0, 5), range(1, 6), range(2, 6))


def mega(
    n_rows,
    n_cols,
    near_count,
    far_count,
    disp_hbm,
    pos_hbm,
    near_pairs_hbm,
    far_pairs_hbm,
    intact_hbm,
    stiffness_hbm,
    basis_hbm,
    far_hbm,
    net_out,
    damage_out,
    ext_disp,
    ext_pos,
    near_pairs,
    far_pairs,
    intact,
    stiffness,
    wide,
    centred,
    left,
    lefts,
    held,
    sums,
    right_q,
    right_s,
    disp_rows,
    pos_rows,
    disp_f,
    pos_f,
    weights,
    near_rows,
    basis,
    far_blocks,
    column,
    coupled,
    partial,
    arrived,
    local_sem,
    halo_send,
    halo_recv,
    gather_send,
    gather_recv,
    scatter_send,
    scatter_recv,
):
    f32, bf16 = jnp.float32, jnp.bfloat16
    i, j = lax.axis_index("rows"), lax.axis_index("cols")
    me = i * n_cols + j
    devices = n_rows * n_cols
    next_id = lax.rem(me + 1, devices)
    last_id = lax.rem(me + devices - 1, devices)
    row_peers = [lax.rem(me + d * n_cols, devices) for d in range(1, n_rows)]
    col_places = [lax.rem(j + d, n_cols) for d in range(1, n_cols)]
    col_peers = [i * n_cols + place for place in col_places]

    own = pl.ds(0, OWN)
    loads = [
        pltpu.make_async_copy(src, dst, local_sem.at[n])
        for n, (src, dst) in enumerate(
            (
                (disp_hbm, ext_disp.at[own, :]),
                (pos_hbm, ext_pos.at[own, :]),
                (near_pairs_hbm, near_pairs),
                (basis_hbm, basis),
                (far_pairs_hbm, far_pairs),
                (intact_hbm, intact),
                (stiffness_hbm, stiffness),
                (far_hbm, far_blocks),
            )
        )
    ]
    for copy in loads:
        copy.start()
    barrier = pltpu.get_barrier_semaphore()
    peers = row_peers + col_peers + [next_id, last_id]
    for peer in peers:
        pl.semaphore_signal(barrier, inc=1, device_id=peer, device_id_type=LOGICAL)

    for n in range(6):
        wide[n, 0:8, :] = jnp.zeros((8, LANES), jnp.float32)
        wide[n, OWN : OWN + 8, :] = jnp.zeros((8, LANES), jnp.float32)
    for copy in loads[:3]:
        copy.wait()

    def lanes_of(c):
        return slice(c * ELEMS, (c + 1) * ELEMS)

    def thirds(x):
        high = x.astype(bf16).astype(f32)
        middle = (x - high).astype(bf16).astype(f32)
        return high, middle, (x - high) - middle

    def square_sum(x):
        return x[0] * x[0] + x[1] * x[1] + x[2] * x[2]

    gap = jnp.zeros((GROUPS, LANES - ELEMS), f32)
    one = jnp.ones((GROUPS, LANES), f32)
    none = jnp.zeros((GROUPS, LANES), f32)

    def rows_of(n, stride):
        return pl.ds(n, GROUPS, stride=stride)

    def block_of(n):
        return slice(GROUPS * n, GROUPS * (n + 1))

    def widen(n, ext, c, halo):
        wide[n, 2 : OWN + 2, 0:ELEMS] = ext[0:OWN, lanes_of(c)]
        if halo:
            wide[n, 0:2, 0:ELEMS] = ext[126:128, lanes_of(c)]
            wide[n, OWN + 2 : OWN + 4, 0:ELEMS] = ext[OWN : OWN + 2, lanes_of(c)]

    def build(halo):
        for c in range(3):
            widen(c, ext_pos, c, halo)
            widen(3 + c, ext_disp, c, halo)
        centre = []
        for c in range(3):
            inner = wide[c, rows_of(3, 4), :][:, :ELEMS] + wide[c, rows_of(4, 4), :][:, :ELEMS]
            centre.append(jnp.sum(inner, axis=1, keepdims=True) * (0.5 / ELEMS))
        if not halo:
            for m in range(4):
                x = [wide[c, rows_of(2 + m, 4), :][:, :ELEMS] - centre[c] for c in range(3)]
                x = [jnp.concatenate([v, gap], axis=1) for v in x]
                parts = [thirds(v) for v in x]
                norm = thirds(square_sum(x))
                for c in range(3):
                    centred[c, rows_of(m, 4), :] = x[c]
                    for n, (a, _) in enumerate(PIECES):
                        left[m, block_of(3 * n + c), :] = parts[c][a]
                for n in range(3):
                    left[m, block_of(18 + n), :] = one
                    left[m, block_of(21 + n), :] = norm[n]

        def packed(n, half):
            a0, a1, a2, a3 = [wide[n, rows_of(4 * half + m, 4), :][:, :ELEMS] for m in range(4)]
            return (
                jnp.concatenate([a0, a1[:, :32]], axis=1),
                jnp.concatenate([a1[:, 32:], a2[:, :64]], axis=1),
                jnp.concatenate([a2[:, 64:], a3], axis=1),
            )

        for half in range(2):
            sources = [packed(n, half) for n in range(6)]
            for v in range(3):
                if halo and v == 2 - 2 * half:
                    continue
                w = 3 * half + v
                y = [sources[c][v] - centre[c] for c in range(3)]
                u = [sources[3 + c][v] for c in range(3)]
                y_parts = [thirds(value) for value in y]
                u_parts = [thirds(value) for value in u]
                norm = thirds(square_sum(y) + core_square)
                inner = thirds(y[0] * u[0] + y[1] * u[1] + y[2] * u[2])
                for c in range(3):
                    for n, (_, b) in enumerate(PIECES):
                        right_q[w, block_of(3 * n + c), :] = -2.0 * y_parts[c][b]
                        right_s[w, block_of(3 * n + c), :] = u_parts[c][b]
                    disp_f[w, block_of(c), :] = u[c]
                    pos_f[w, block_of(c), :] = 3.0 * y[c]
                    triple = thirds(3.0 * y[c])
                    for n in range(2):
                        disp_rows[w, block_of(4 * n + c), :] = u_parts[c][n]
                        pos_rows[w, block_of(4 * n + c), :] = triple[n]
                for n in range(3):
                    right_q[w, block_of(18 + n), :] = norm[n]
                    right_s[w, block_of(18 + n), :] = -inner[n]
                    right_q[w, block_of(21 + n), :] = one
                    right_s[w, block_of(21 + n), :] = none
                for n in (3, 7):
                    disp_rows[w, block_of(n), :] = none
                    pos_rows[w, block_of(n), :] = 3.0 * one if n == 3 else none

    build(False)

    slots = near_pairs.shape[1]
    near_target = near_pairs[0:1, :]
    live = lax.broadcasted_iota(jnp.int32, (1, slots), 1) < near_count[0]
    place = near_pairs[1:2, :] - near_target // 4 * 4
    row_is = lax.broadcasted_iota(jnp.int32, (OWN, slots), 0) == jnp.where(live, near_target, -1)
    lane_is = lax.broadcasted_iota(jnp.int32, (8 * ELEMS, slots), 0) // ELEMS == place
    row_is = row_is.astype(f32).astype(bf16)
    for w in range(6):
        weights[w] = lax.dot_general(
            row_is,
            lane_is[w * LANES : (w + 1) * LANES].astype(f32).astype(bf16),
            (((1,), (1,)), ((), ())),
            preferred_element_type=f32,
        )

    def halves(x):
        high = x.astype(bf16)
        return high, (x - high.astype(f32)).astype(bf16)

    def turn(g):
        for m in range(4):
            lefts[4 * g + m] = left[m, pl.ds(g, 24, stride=GROUPS), :].T[:ELEMS].astype(bf16)

    def settle(g):
        for m in range(4):
            row = pl.ds(4 * g + m, 1)
            total = sums[4 * g + m].T
            total = total[0:4] + total[4:8]
            for c in range(3):
                near_rows[c, row, 0:ELEMS] = total[c : c + 1] - centred[c, row, 0:ELEMS] * total[3:4]

    def meet(g, w):
        group = pl.ds(g, 24, stride=GROUPS)
        right = jnp.concatenate([right_q[w, group, :], right_s[w, group, :]], axis=1).astype(bf16)
        seen = [m for m in range(4) if w in SEEN[m]]
        mine = jnp.concatenate([lefts[4 * g + m] for m in seen], axis=0)
        both = jnp.dot(mine, right, preferred_element_type=f32)
        for at, m in enumerate(seen):
            held[6 * m + w] = both[at * ELEMS : (at + 1) * ELEMS]

    def near_groups(first, last):
        def near_group(t, _):
            g = lax.rem(t + 1, GROUPS)
            eight = pl.ds(g, 8, stride=GROUPS)
            rows = []
            for w in range(6):
                u_rows = disp_rows[w, eight, :].astype(bf16)
                y_rows = pos_rows[w, eight, :].astype(bf16)
                rows.append(jnp.concatenate([u_rows, u_rows, y_rows, y_rows], axis=1))
            totals = [None] * 4
            plain = {m: [jnp.zeros((ELEMS, LANES), f32)] * 4 for m in PLAIN}
            for n in range(5):
                for pair in range(2):
                    w = n + pair
                    seen = [m for m in (2 * pair, 2 * pair + 1) if w in SEEN[m]]
                    values = []
                    for m in seen:
                        part = held[6 * m + w]
                        inverse = lax.rsqrt(jnp.maximum(part[:, :LANES], core_square))
                        square = inverse * inverse
                        cube = square * (inverse * weights[w, pl.ds(4 * g + m, 1), :])
                        pull = (part[:, LANES:] * square) * cube
                        if m in PLAIN:
                            u = [disp_f[w, pl.ds(GROUPS * c + g, 1), :] for c in range(3)]
                            y = [pos_f[w, pl.ds(GROUPS * c + g, 1), :] for c in range(3)]
                            plain[m] = [plain[m][c] + (cube * u[c] + pull * y[c]) for c in range(3)] + [plain[m][3] + pull]
                        else:
                            values.append(jnp.concatenate(halves(cube) + halves(pull), axis=1))
                    seen = [m for m in seen if m not in PLAIN]
                    if not seen:
                        continue
                    added = lax.dot_general(
                        jnp.concatenate(values, axis=0), rows[w], (((1,), (1,)), ((), ())), preferred_element_type=f32
                    )
                    for at, m in enumerate(seen):
                        piece = added[at * ELEMS : (at + 1) * ELEMS]
                        totals[m] = piece if totals[m] is None else totals[m] + piece
                meet(lax.rem(t + 2, GROUPS), n)
            meet(lax.rem(t + 2, GROUPS), 5)
            lane = lax.broadcasted_iota(jnp.int32, (ELEMS, 8), 1)
            for m in PLAIN:
                columns = [jnp.sum(x, axis=1, keepdims=True) for x in plain[m]]
                columns[3] = 3.0 * columns[3]
                total = jnp.zeros((ELEMS, 8), f32)
                for c in range(4):
                    total = jnp.where(lane == c, columns[c], total)
                totals[m] = total
            settle(t)
            for m in range(4):
                sums[4 * g + m] = totals[m]
            turn(lax.rem(t + 3, GROUPS))
            return 0

        lax.fori_loop(first, last, near_group, 0)
        settle(lax.rem(last, GROUPS))

    turn(1)
    turn(2)
    for w in range(6):
        meet(1, w)

    loads[3].wait()

    def project(block, coeff):
        top = pl.multiple_of(block * 8, 8)
        rows = ext_disp[pl.ds(top, 8), :].astype(bf16)
        lane = lax.broadcasted_iota(jnp.int32, (RANK, OWN), 1)
        for n in range(8):
            product = basis[top + n] * rows[n : n + 1, :]
            product = product[:, :LANES].astype(f32) + product[:, LANES : 2 * LANES].astype(f32) + jnp.concatenate(
                [product[:, 2 * LANES :].astype(f32), jnp.zeros((RANK, 3 * LANES - WIDTH), f32)], axis=1
            )
            coeff = jnp.where(lane == top + n, jnp.sum(product, axis=1, keepdims=True), coeff)
        return coeff

    coeff = lax.fori_loop(0, OWN // 8, project, jnp.zeros((RANK, OWN), f32))
    half = OWN // 2

    def pack(block):
        return jnp.concatenate([block[:half], block[half:]], axis=1).astype(bf16)

    own_rows = pl.ds(pl.multiple_of(i * half, half), half)
    column[own_rows, :] = pack(coeff)

    z = lax.rem(j, 4) * 2 + i // (n_rows // 2)
    sent = jnp.where(z == 0, 8, jnp.where(z == 1, 6, jnp.where(z == 2, 4, jnp.where(z == 3, 3, 0))))
    gathered_at = sent + jnp.where(z == 1, 6, 5)
    near_groups(0, sent)
    pl.semaphore_wait(barrier, len(peers))

    def remote(src, dst, send, recv, peer):
        return pltpu.make_async_remote_copy(
            src_ref=src, dst_ref=dst, send_sem=send, recv_sem=recv, device_id=peer, device_id_type=LOGICAL
        )

    mine = column.at[own_rows, :]
    gathers = [
        remote(mine, mine, gather_send.at[d], gather_recv.at[d], peer) for d, peer in enumerate(row_peers)
    ]
    halos = []
    for n, (src, dst) in enumerate(((disp_hbm, ext_disp), (pos_hbm, ext_pos))):
        halos.append(remote(src.at[pl.ds(OWN - 8, 8), :], dst.at[pl.ds(120, 8), :], halo_send.at[n], halo_recv.at[n], next_id))
        halos.append(remote(src.at[pl.ds(0, 8), :], dst.at[pl.ds(OWN, 8), :], halo_send.at[2 + n], halo_recv.at[2 + n], last_id))
    for copy in gathers + halos:
        copy.start()

    near_groups(sent, gathered_at)

    for copy in gathers:
        copy.wait()
    for copy in loads[4:]:
        copy.wait()
    tops = [column[n * half : (n + 1) * half, :RANK] for n in range(n_rows)]
    bottoms = [column[n * half : (n + 1) * half, RANK:] for n in range(n_rows)]
    column_turned = jnp.concatenate(
        [jnp.concatenate(tops, axis=1), jnp.concatenate(bottoms, axis=1)], axis=0
    )
    far_slots = far_pairs.shape[1]
    sources = n_rows * OWN

    wide_block = 2 * LANES
    sublane = lax.broadcasted_iota(jnp.int32, (8, wide_block), 0)

    def merge(blocks):
        reach = 4
        while len(blocks) > 1:
            upper = sublane // reach % 2 == 0
            count = len(blocks) // 2
            pairs = [(blocks[n], blocks[n + count]) for n in range(count)]
            blocks = []
            for x, y in pairs:
                crossed = jnp.where(upper, y, x)
                moved = pltpu.roll(crossed, reach, axis=0)
                if reach < 4:
                    moved = jnp.where(upper, pltpu.roll(crossed, 8 - reach, axis=0), moved)
                blocks.append(jnp.where(upper, x, y) + moved)
            reach //= 2
        return blocks[0]

    def couple(block, _):
        first = pl.multiple_of(block * wide_block, wide_block)
        source = far_pairs[1:2, pl.ds(first, wide_block)]
        alive = lax.broadcasted_iota(jnp.int32, (1, wide_block), 1) + first < far_count[0]
        source = jnp.where(alive, source, -1)
        chosen = (lax.broadcasted_iota(jnp.int32, (sources, wide_block), 0) == source).astype(f32).astype(bf16)
        gathered = jnp.dot(column_turned, chosen, preferred_element_type=f32).astype(bf16)

        def ranks(part, _):
            top = pl.multiple_of(part * 16, 16)
            summed = []
            for n in range(16):
                product = far_blocks[top + n, :, pl.ds(first, wide_block)] * gathered
                product = ((product[0:16] + product[16:32]) + (product[32:48] + product[48:64])).astype(f32)
                summed.append(product[0:8] + product[8:16])
            whole = jnp.concatenate([merge(summed[:8]), merge(summed[8:])], axis=0)
            coupled[pl.ds(top, 16), pl.ds(first, wide_block)] = whole.astype(bf16)
            return 0

        return lax.fori_loop(0, RANK // 16, ranks, 0)

    lax.fori_loop(0, far_slots // wide_block, couple, 0)

    def collect(block, _):
        first = pl.multiple_of(block * wide_block, wide_block)
        chosen = lax.broadcasted_iota(jnp.int32, (wide_block, far_slots), 0) + first == far_pairs[0:1, :]
        found = lax.dot_general(
            chosen.astype(f32).astype(bf16), coupled[...], (((1,), (1,)), ((), ())), preferred_element_type=f32
        )
        for n in range(wide_block // OWN):
            to = pl.multiple_of(block * (wide_block // 2) + n * half, half)
            partial[pl.ds(to, half), :] = pack(found[n * OWN : (n + 1) * OWN])
        return 0

    lax.fori_loop(0, n_cols * OWN // wide_block, collect, 0)

    for copy in halos:
        copy.wait()

    here = pl.ds(pl.multiple_of(j * half, half), half)
    scatters = []
    for d, peer in enumerate(col_peers):
        block = partial.at[pl.ds(pl.multiple_of(col_places[d] * half, half), half), :]
        scatters.append(remote(block, arrived.at[here, :], scatter_send.at[d], scatter_recv.at[d], peer))
    for copy in scatters:
        copy.start()
    arrived[here, :] = partial[here, :]

    ext_disp[OWN : OWN + 8, :] = jnp.where(me == devices - 1, 0.0, ext_disp[OWN : OWN + 8, :])
    ext_disp[120:128, :] = jnp.where(me == 0, 0.0, ext_disp[120:128, :])
    build(True)
    near_groups(gathered_at, GROUPS)

    parts = [near_rows[c, :, 0:ELEMS] for c in range(3)]
    u = [ext_disp[0:OWN, lanes_of(c)] for c in range(3)]
    separation = jnp.sqrt(1.0 + (u[0] * u[0] + u[1] * u[1] + u[2] * u[2]))
    softened = 1.0 - jnp.exp(-(separation - 1.0) / softening)
    whole_element = intact[...].astype(f32)
    damage = whole_element * softened + (1.0 - whole_element)
    damage_out[...] = damage
    held = (1.0 - damage) * stiffness[...]
    base = jnp.concatenate([parts[c] - held * u[c] for c in range(3)], axis=1)

    for copy in scatters:
        copy.wait()
    owned = arrived[0:half, :].astype(f32)
    for n in range(1, n_cols):
        owned = owned + arrived[n * half : (n + 1) * half, :].astype(f32)
    owned = owned.T
    owned = jnp.concatenate([owned[:RANK], owned[RANK:]], axis=1)
    fold = lax.broadcasted_iota(jnp.int32, (16, 256), 0) == lax.broadcasted_iota(jnp.int32, (16, 256), 1) // 16
    fold = fold.astype(f32).astype(bf16)
    for block in range(OWN // 16):
        summed = []
        for n in range(16):
            k = 16 * block + n
            product = basis[k] * owned[:, k : k + 1].astype(bf16)
            summed.append((product[0:16] + product[16:32]) + (product[32:48] + product[48:64]))
        far = jnp.dot(fold, jnp.concatenate(summed, axis=0), preferred_element_type=f32)
        net_out[16 * block : 16 * block + 16, :] = base[16 * block : 16 * block + 16] + far


def local(
    displacement,
    positions,
    cluster_basis,
    near_pairs,
    near_count,
    far_pairs,
    far_count,
    far_blocks,
    intact,
    stiffness,
):
    n_rows, n_cols = lax.axis_size("rows"), lax.axis_size("cols")
    f32, bf16 = jnp.float32, jnp.bfloat16
    far_slots = far_pairs.shape[0]
    vmem = pl.BlockSpec(memory_space=pltpu.VMEM)
    smem = pl.BlockSpec(memory_space=pltpu.SMEM)
    hbm = pl.BlockSpec(memory_space=pltpu.HBM)
    return pl.pallas_call(
        functools.partial(mega, n_rows, n_cols),
        out_shape=(
            jax.ShapeDtypeStruct((OWN, WIDTH), f32),
            jax.ShapeDtypeStruct((OWN, ELEMS), f32),
        ),
        in_specs=[smem] * 2 + [hbm] * 8,
        out_specs=(vmem, vmem),
        scratch_shapes=[
            pltpu.VMEM((2 * OWN, WIDTH), f32),
            pltpu.VMEM((2 * OWN, WIDTH), f32),
            pltpu.VMEM((2, near_pairs.shape[0]), jnp.int32),
            pltpu.VMEM((2, far_slots), jnp.int32),
            pltpu.VMEM((OWN, ELEMS), jnp.int32),
            pltpu.VMEM((OWN, ELEMS), f32),
            pltpu.VMEM((6, OWN + 8, LANES), f32),
            pltpu.VMEM((3, OWN, LANES), f32),
            pltpu.VMEM((4, 24 * GROUPS, LANES), f32),
            pltpu.VMEM((OWN, ELEMS, 24), bf16),
            pltpu.VMEM((24, ELEMS, 2 * LANES), f32),
            pltpu.VMEM((OWN, ELEMS, 8), f32),
            pltpu.VMEM((6, 24 * GROUPS, LANES), f32),
            pltpu.VMEM((6, 24 * GROUPS, LANES), f32),
            pltpu.VMEM((6, 8 * GROUPS, LANES), f32),
            pltpu.VMEM((6, 8 * GROUPS, LANES), f32),
            pltpu.VMEM((6, 3 * GROUPS, LANES), f32),
            pltpu.VMEM((6, 3 * GROUPS, LANES), f32),
            pltpu.VMEM((6, OWN, LANES), f32),
            pltpu.VMEM((3, OWN, LANES), f32),
            pltpu.VMEM((OWN, RANK, WIDTH), bf16),
            pltpu.VMEM((RANK, RANK, far_slots), bf16),
            pltpu.VMEM((n_rows * OWN // 2, 2 * RANK), bf16),
            pltpu.VMEM((RANK, far_slots), bf16),
            pltpu.VMEM((n_cols * OWN // 2, 2 * RANK), bf16),
            pltpu.VMEM((n_cols * OWN // 2, 2 * RANK), bf16),
            pltpu.SemaphoreType.DMA((8,)),
            pltpu.SemaphoreType.DMA((4,)),
            pltpu.SemaphoreType.DMA((4,)),
            pltpu.SemaphoreType.DMA((n_rows - 1,)),
            pltpu.SemaphoreType.DMA((n_rows - 1,)),
            pltpu.SemaphoreType.DMA((n_cols - 1,)),
            pltpu.SemaphoreType.DMA((n_cols - 1,)),
        ],
        compiler_params=pltpu.CompilerParams(
            collective_id=0, has_side_effects=True, vmem_limit_bytes=40 * 1024 * 1024
        ),
        name="traction",
    )(
        near_count,
        far_count,
        *[
            pltpu.with_memory_space_constraint(x, pltpu.HBM)
            for x in (
                displacement,
                positions,
                near_pairs.T,
                far_pairs.T,
                intact,
                stiffness,
                jnp.transpose(cluster_basis, (0, 2, 1)),
                jnp.transpose(far_blocks, (1, 2, 0)),
            )
        ],
    )


def solution(mesh):
    both = ("rows", "cols")
    in_specs = (
        P(both, None),
        P(both, None),
        P(both, None, None),
        P(both, None),
        P(both),
        P(both, None),
        P(both),
        P(both, None, None),
        P(both, None),
        P(both, None),
    )
    out_specs = (P(both, None), P(both, None))
    return jax.shard_map(local, mesh=mesh, in_specs=in_specs, out_specs=out_specs, check_vma=False)
```
